128 devices in a mesh: gx: 8 (over z_hi, y), gy: 8 (over z_lo, x), gz: 2 (over core).
Axes of the slice: x: 4, y: 4, z: 4 (z_hi: 2, z_lo: 2; z = z_hi * 2 + z_lo), core: 2. Of those that a mesh axis runs over, the one named last changes fastest.
Arguments:
- state: bfloat16 [32, 128, 128, 256], P('gx', ('gy', 'gz')), may hold values from -6 to 6
- cotangent: bfloat16 [32, 128, 128, 256], P('gx', ('gy', 'gz')), may hold values from -6 to 6
- factors: bfloat16 [262144, 256], P(('gx', 'gy', 'gz')), may hold values from -0.25 to 0.25
- speeds: float32 [3, 262144], P(None, ('gx', 'gy', 'gz')), may hold values from 0.25 to 4
- signs: int32 [3, 262144], P(None, ('gx', 'gy', 'gz')), may hold values from 0 to 1, as said below
- mask: int32 [32, 128, 128], P('gx', ('gy', 'gz')), may hold values 0 or 1
Outputs:
- grad_state: bfloat16 [32, 128, 128, 256], P('gx', ('gy', 'gz'))
- grad_factors: float32 [262144, 256], P(('gx', 'gy', 'gz'))
The draws below stay inside these ranges and needn't reach their ends.
Inputs may be any that keep to these rules, and one draw needn't show every extreme that they name: `signs`: 1 where the velocity component points towards higher indices, else 0. `mask`: 1 where a cell is updated, 0 where it is held fixed.
All inputs are finite; a program needn't handle non-finite values. No bound on the sum of `mask` on one device may be relied on, other than what follows from the above.
Results may differ from the reference program's by a relative error of at most 0.0068.
Values may be sent and summed in bfloat16 or wider, within the bound.
No kernel may reach another device: no remote copies, remote signals or barrier semaphores. Data moves between devices by JAX's collectives and lax.ppermute only.
A program may use at most 128 MiB of HBM per device.

```python
import math
import jax
import jax.numpy as jnp
from jax import lax

R = 256
NZ = 128
NX = 32
NY = 128
NV = 262144


def sign_table(key):
    return jax.random.randint(jax.random.fold_in(key, 11), (3, NV), 0, 2).astype(jnp.int32)


def draw_signs(key, part):
    return sign_table(key)


def draw_factors(key, part):
    streams = jax.random.split(jax.random.fold_in(key, 23), 5)
    base_rows = jax.random.normal(streams[0], (NV, R), jnp.float32)
    common_mix = jax.random.normal(streams[1], (R, R), jnp.float32) / math.sqrt(R)
    mixed = base_rows + 0.35 * jnp.dot(base_rows, common_mix)
    signed = 2.0 * sign_table(key).astype(jnp.float32) - 1.0
    for direction in range(3):
        mixing = jax.random.normal(streams[2 + direction], (R, R), jnp.float32) / math.sqrt(R)
        mixed = mixed + 0.25 * jnp.dot(signed[direction][:, None] * base_rows, mixing)
    return jnp.clip(0.7 * mixed / math.sqrt(NV), -0.25, 0.25).astype(jnp.bfloat16)


def draw_speeds(key, part):
    stream = jax.random.fold_in(key, 37)
    position = jnp.arange(NV, dtype=jnp.float32) / NV
    spread = jnp.exp(jax.random.uniform(stream, (3, NV), jnp.float32, -math.log(2.0), math.log(2.0)))
    return 0.5 * jnp.exp(math.log(4.0) * position)[None, :] * spread


def touch_ends(drawn, rng, low, largest):
    index_at = [jax.random.randint(jax.random.fold_in(rng, axis), (), 0, length) for axis, length in enumerate(drawn.shape)]
    main_axis = drawn.shape.index(max(drawn.shape))
    neighbour = index_at[:main_axis] + [(index_at[main_axis] + 1) % drawn.shape[main_axis]] + index_at[main_axis + 1:]
    return drawn.at[tuple(index_at)].set(low).at[tuple(neighbour)].set(largest)


def level_of(own_key, shape, cuts, low, largest):
    factor_of, own = 1.0, jax.random.fold_in(own_key, 6)
    for dim, blocks in cuts:
        steps = jnp.exp(jax.random.uniform(jax.random.fold_in(own, dim), (blocks,), jnp.float32, low / len(cuts), largest / len(cuts)))
        factor_of = factor_of * jnp.repeat(steps, shape[dim] // blocks).reshape([-1 if axis == dim else 1 for axis in range(len(shape))])
    return factor_of


def noise(key, shape, deviation, limit, cuts=(), kind=jnp.bfloat16):
    entries = jax.random.normal(key, shape, jnp.float32) * deviation
    if len(cuts) > 0:
        entries = level_of(key, shape, cuts, -0.22, 0.18) * entries
    return jnp.clip(entries, min=-limit, max=limit).astype(kind)


def setup_inputs(seed: int = 0) -> dict:
    streams_of = jax.random.split(jax.random.key(seed), 7)
    state = noise(streams_of[0], (NX, NY, NZ, R), 1.0, 6.0, ((0, 8), (1, 16)))
    cotangent = noise(streams_of[1], (NX, NY, NZ, R), 1.0, 6.0, ((0, 8), (1, 16)))
    factors = draw_factors(jax.random.fold_in(streams_of[6], 71), 0)
    speeds = draw_speeds(jax.random.fold_in(streams_of[6], 71), 0)
    signs = draw_signs(jax.random.fold_in(streams_of[6], 71), 0)
    mask = touch_ends((jax.random.randint(streams_of[5], (NX, NY, NZ), 0, 8) < 7).astype(jnp.int32), jax.random.fold_in(streams_of[5], 1), 0, 1)
    return {"state": state, "cotangent": cotangent, "factors": factors, "speeds": speeds, "signs": signs, "mask": mask}


courant = 0.2


def differences(grid_field, direction):
    values = grid_field.astype(jnp.float32)
    extent = values.shape[direction]
    zero_face = jnp.zeros_like(lax.slice_in_dim(values, 0, 1, axis=direction))
    before = jnp.concatenate([zero_face, lax.slice_in_dim(values, 0, extent - 1, axis=direction)], axis=direction)
    following = jnp.concatenate([lax.slice_in_dim(values, 1, extent, axis=direction), zero_face], axis=direction)
    return (values - before).astype(jnp.bfloat16), (following - values).astype(jnp.bfloat16)


def flatten_cells(grid_field):
    return grid_field.reshape(-1, grid_field.shape[-1])


def contract_cells(left_side, right_side):
    return lax.dot_general(left_side, right_side, (((0,), (0,)), ((), ())), preferred_element_type=jnp.float32)


def build_rates(speeds, signs):
    chosen = signs.astype(jnp.float32)
    rate_rows = []
    for direction in range(3):
        rate_rows.append(speeds[direction] * chosen[direction])
        rate_rows.append(speeds[direction] * (1.0 - chosen[direction]))
    return jnp.stack(rate_rows)


def backward_terms(held_field, partner, flux_bf):
    grid_shape = held_field.shape
    running = jnp.zeros(grid_shape, jnp.float32)
    flat_partner = flatten_cells(partner)
    flux_grads = []
    for direction in range(3):
        lower_diff, upper_diff = differences(held_field, direction)
        lower_flat = flatten_cells(lower_diff)
        upper_flat = flatten_cells(upper_diff)
        term = jnp.dot(upper_flat, flux_bf[2 * direction].T, preferred_element_type=jnp.float32) - jnp.dot(lower_flat, flux_bf[2 * direction + 1].T, preferred_element_type=jnp.float32)
        running = running + courant * term.reshape(grid_shape)
        flux_grads.append(contract_cells(flat_partner, upper_flat))
        flux_grads.append(contract_cells(flat_partner, lower_flat))
    return running, flux_grads


def reference(state, cotangent, factors, speeds, signs, mask):
    rate_table = build_rates(speeds, signs)
    values = factors.astype(jnp.float32)
    flux_list = []
    for which_rate in range(6):
        weighted = (rate_table[which_rate][:, None] * values).astype(jnp.bfloat16)
        flux_list.append(contract_cells(factors, weighted))
    flux_bf = jnp.stack(flux_list).astype(jnp.bfloat16)
    grid_shape = state.shape
    cell_gate = mask.astype(jnp.float32)[..., None]
    flow_term = jnp.zeros(grid_shape, jnp.float32)
    for direction in range(3):
        lower_diff, upper_diff = differences(state, direction)
        term = jnp.dot(flatten_cells(lower_diff), flux_bf[2 * direction], preferred_element_type=jnp.float32) - jnp.dot(flatten_cells(upper_diff), flux_bf[2 * direction + 1], preferred_element_type=jnp.float32)
        flow_term = flow_term - courant * term.reshape(grid_shape)
    middle = (state.astype(jnp.float32) + cell_gate * flow_term).astype(jnp.bfloat16)
    held_back = cotangent * mask.astype(jnp.bfloat16)[..., None]
    back_held, grads_held = backward_terms(held_back, middle, flux_bf)
    inner_grad = 0.5 * cotangent.astype(jnp.float32) + 0.5 * back_held
    held_inner = (cell_gate * inner_grad).astype(jnp.bfloat16)
    back_inner, grads_inner = backward_terms(held_inner, state, flux_bf)
    grad_state = (0.5 * cotangent.astype(jnp.float32) + inner_grad + back_inner).astype(jnp.bfloat16)
    flux_grad = []
    for direction in range(3):
        flux_grad.append(courant * (grads_inner[2 * direction] + 0.5 * grads_held[2 * direction]))
        flux_grad.append(-courant * (grads_inner[2 * direction + 1] + 0.5 * grads_held[2 * direction + 1]))
    flux_grad = jnp.stack(flux_grad)
    symmetric = (flux_grad + jnp.swapaxes(flux_grad, 1, 2)).astype(jnp.bfloat16)
    grad_factors = jnp.zeros(factors.shape, jnp.float32)
    for which_rate in range(6):
        weighted = (rate_table[which_rate][:, None] * values).astype(jnp.bfloat16)
        grad_factors = grad_factors + jnp.dot(weighted, symmetric[which_rate], preferred_element_type=jnp.float32)
    return grad_state, grad_factors
```

```python
import jax
import jax.numpy as jnp
from jax import lax
from jax.sharding import PartitionSpec as P

courant = 0.2


def with_halo(block, sides, width):
    for axis, dim in sides:
        count = lax.axis_size(axis)
        forward = [(i, i + 1) for i in range(count - 1)]
        backward = [(target, source) for source, target in forward]
        low = lax.ppermute(
            lax.slice_in_dim(block, block.shape[dim] - width, None, axis=dim), axis, forward
        )
        high = lax.ppermute(lax.slice_in_dim(block, 0, width, axis=dim), axis, backward)
        block = jnp.concatenate([low, block, high], axis=dim)
    return block


def sum_everywhere(partial, axes):
    shape = partial.shape
    count = 1
    for axis in axes:
        count *= lax.axis_size(axis)
    pieces = partial.astype(jnp.bfloat16).reshape(count, -1, 128)
    mine = lax.all_to_all(pieces, axes, split_axis=0, concat_axis=0, tiled=True)
    total = jnp.sum(mine.astype(jnp.float32), axis=0).astype(jnp.bfloat16)
    copies = jnp.broadcast_to(total[None], pieces.shape)
    whole = lax.all_to_all(copies, axes, split_axis=0, concat_axis=0, tiled=True)
    return whole.reshape(shape)


def build_rates(speeds, signs):
    chosen = signs.astype(jnp.float32)
    rate_rows = []
    for direction in range(3):
        rate_rows.append(speeds[direction] * chosen[direction])
        rate_rows.append(speeds[direction] * (1.0 - chosen[direction]))
    return jnp.stack(rate_rows)


def neighbour_pairs(padded):
    centre = padded[1:-1, 1:-1].astype(jnp.float32)
    rank_size = centre.shape[-1]
    zero_face = jnp.zeros_like(centre[:, :, :1])
    sides = (
        (padded[:-2, 1:-1], padded[2:, 1:-1]),
        (padded[1:-1, :-2], padded[1:-1, 2:]),
        (
            jnp.concatenate([zero_face, centre[:, :, :-1]], axis=2),
            jnp.concatenate([centre[:, :, 1:], zero_face], axis=2),
        ),
    )
    diff_pairs = []
    for lower_side, upper_side in sides:
        lower_diff = (centre - lower_side.astype(jnp.float32)).astype(jnp.bfloat16)
        upper_diff = (upper_side.astype(jnp.float32) - centre).astype(jnp.bfloat16)
        diff_pairs.append(
            jnp.concatenate([lower_diff, upper_diff], axis=-1).reshape(-1, 2 * rank_size)
        )
    return diff_pairs


def backward_terms(diff_pairs, partner, back_mats):
    grid_shape = partner.shape
    flat_partner = partner.reshape(-1, grid_shape[-1])
    running = None
    flux_grads = []
    for direction in range(3):
        term = jnp.dot(
            diff_pairs[direction], back_mats[direction], preferred_element_type=jnp.float32
        )
        running = term if direction == 0 else running + term
        flux_grads.append(
            lax.dot_general(
                flat_partner,
                diff_pairs[direction],
                (((0,), (0,)), ((), ())),
                preferred_element_type=jnp.float32,
            )
        )
    return (courant * running.reshape(grid_shape), flux_grads)


def on_device(state, cotangent, factors, speeds, signs, mask):
    grid_shape = state.shape
    rank_size = grid_shape[-1]
    rate_table = build_rates(speeds, signs)
    weighted = (rate_table[:, :, None] * factors.astype(jnp.float32)[None]).astype(jnp.bfloat16)
    gram_local = jnp.einsum("vj,kvl->kjl", factors, weighted, preferred_element_type=jnp.float32)
    flux_bf = sum_everywhere(gram_local, ("gx", "gy", "gz"))
    cell_gate = mask.astype(jnp.float32)[..., None]
    held_back = cotangent * mask.astype(jnp.bfloat16)[..., None]
    padded_state = with_halo(state, (("gx", 0), (("gy", "gz"), 1)), 1)
    padded_held = with_halo(held_back, (("gx", 0), (("gy", "gz"), 1)), 1)
    forward_mats = [
        jnp.concatenate([flux_bf[2 * direction], -flux_bf[2 * direction + 1]], axis=0)
        for direction in range(3)
    ]
    back_mats = [
        jnp.concatenate([-flux_bf[2 * direction + 1].T, flux_bf[2 * direction].T], axis=0)
        for direction in range(3)
    ]
    state_pairs = neighbour_pairs(padded_state)
    flow_term = None
    for direction in range(3):
        term = jnp.dot(
            state_pairs[direction], forward_mats[direction], preferred_element_type=jnp.float32
        )
        flow_term = term if direction == 0 else flow_term + term
    flow_term = -courant * flow_term.reshape(grid_shape)
    middle = (state.astype(jnp.float32) + cell_gate * flow_term).astype(jnp.bfloat16)
    back_held, grads_held = backward_terms(neighbour_pairs(padded_held), middle, back_mats)
    inner_grad = 0.5 * cotangent.astype(jnp.float32) + 0.5 * back_held
    held_inner = (cell_gate * inner_grad).astype(jnp.bfloat16)
    padded_inner = with_halo(held_inner, (("gx", 0), (("gy", "gz"), 1)), 1)
    back_inner, grads_inner = backward_terms(neighbour_pairs(padded_inner), state, back_mats)
    grad_state = (0.5 * cotangent.astype(jnp.float32) + inner_grad + back_inner).astype(
        jnp.bfloat16
    )
    flux_grad = []
    for direction in range(3):
        flux_grad.append(
            courant
            * (grads_inner[direction][:, rank_size:] + 0.5 * grads_held[direction][:, rank_size:])
        )
        flux_grad.append(
            -courant
            * (grads_inner[direction][:, :rank_size] + 0.5 * grads_held[direction][:, :rank_size])
        )
    local_grad = jnp.stack(flux_grad)
    symmetric = sum_everywhere(
        local_grad + jnp.swapaxes(local_grad, 1, 2), ("gx", "gy", "gz")
    )
    grad_factors = jnp.einsum(
        "kvj,kjl->vl", weighted, symmetric, preferred_element_type=jnp.float32
    )
    return (grad_state, grad_factors)


def solution(mesh):
    placed = (
        P("gx", ("gy", "gz"), None, None),
        P("gx", ("gy", "gz"), None, None),
        P(("gx", "gy", "gz"), None),
        P(None, ("gx", "gy", "gz")),
        P(None, ("gx", "gy", "gz")),
        P("gx", ("gy", "gz"), None),
    )
    return jax.shard_map(
        on_device,
        mesh=mesh,
        in_specs=placed,
        out_specs=(P("gx", ("gy", "gz"), None, None), P(("gx", "gy", "gz"), None)),
        check_vma=False,
    )
```

```python
import jax
import jax.numpy as jnp
from jax import lax
from jax.experimental import pallas as pl
from jax.experimental.pallas import tpu as pltpu
from jax.sharding import PartitionSpec as P

courant = 0.2
ALL = ("gx", "gy", "gz")
BF = jnp.bfloat16
F32 = jnp.float32
NX, NY, NZ, R = 4, 8, 128, 256
ROWS = NY * NZ
VMEM_LIMIT = 56 * 1024 * 1024
whole = pl.BlockSpec(memory_space=pltpu.VMEM)
raw = pl.BlockSpec(memory_space=pl.ANY)


def params(**kw):
    return pltpu.CompilerParams(vmem_limit_bytes=VMEM_LIMIT, **kw)


def cost(flops, bytes_accessed):
    return pl.CostEstimate(flops=flops, bytes_accessed=bytes_accessed, transcendentals=0)


def tri_masks():
    row = lax.broadcasted_iota(jnp.int32, (128, 128), 0)
    col = lax.broadcasted_iota(jnp.int32, (128, 128), 1)
    return row, col


def store_packed(out_ref, k, a, b, d):
    row, col = tri_masks()
    out_ref[k * 256 : k * 256 + 128, :] = jnp.where(row <= col, a, d).astype(BF)
    out_ref[k * 256 + 128 : k * 256 + 256, :] = b.astype(BF)
    return jnp.sum(jnp.where(row == col, d, 0.0), axis=0, keepdims=True)


def store_diagonals(out_ref, diagonals):
    zeros = jnp.zeros((10, 128), F32)
    out_ref[1536:1552, :] = jnp.concatenate(diagonals + [zeros], axis=0).astype(BF)
    out_ref[1552:2048, :] = jnp.zeros((496, 128), BF)


def load_packed(packed_ref, k):
    row, col = tri_masks()
    t = packed_ref[k * 256 : k * 256 + 128, :].astype(F32)
    b = packed_ref[k * 256 + 128 : k * 256 + 256, :].astype(F32)
    diag = packed_ref[1536:1552, :].astype(F32)[k : k + 1, :]
    tt = t.T
    a = jnp.where(row <= col, t, tt)
    d = jnp.where(row > col, t, jnp.where(row < col, tt, jnp.broadcast_to(diag, (128, 128))))
    return a, b, b.T, d


def rate_rows(speeds_ref, signs_ref):
    rows = []
    for d in range(3):
        chosen = signs_ref[d : d + 1, :].astype(F32)
        speed = speeds_ref[d : d + 1, :]
        rows.append(speed * chosen)
        rows.append(speed * (1.0 - chosen))
    return rows


def gram_kernel(factors_ref, speeds_ref, signs_ref, out_ref, turned_ref, acc_ref):
    rows = rate_rows(speeds_ref, signs_ref)
    turned = factors_ref[...].astype(F32).T
    for k in range(6):
        turned_ref[k * 256 : k * 256 + 256, :] = (turned * rows[k]).astype(BF)
    acc_ref[...] = jnp.dot(turned_ref[...], factors_ref[...], preferred_element_type=F32)
    diagonals = []
    for k in range(6):
        g = acc_ref.at[pl.ds(k * 256, 256), :]
        diagonals.append(
            store_packed(out_ref, k, g[:128, :128], g[:128, 128:], g[128:, 128:])
        )
    store_diagonals(out_ref, diagonals)


def gram(factors, speeds, signs):
    return pl.pallas_call(
        gram_kernel,
        out_shape=jax.ShapeDtypeStruct((2048, 128), BF),
        in_specs=[whole] * 3,
        out_specs=whole,
        scratch_shapes=[pltpu.VMEM((1536, 2048), BF), pltpu.VMEM((1536, 256), F32)],
        compiler_params=params(),
        cost_estimate=cost(2 * 2048 * 256 * 1536, 2 << 20),
        name="gram",
    )(factors, speeds, signs)


def total_kernel(parts_ref, out_ref):
    total = jnp.sum(parts_ref[...].astype(F32), axis=0).astype(BF)
    out_ref[...] = jnp.broadcast_to(total[None], (128, 16, 128))


def sum_everywhere(packed):
    pieces = packed.reshape(128, 16, 128)
    mine = lax.all_to_all(pieces, ALL, split_axis=0, concat_axis=0, tiled=True)
    copies = pl.pallas_call(
        total_kernel,
        out_shape=jax.ShapeDtypeStruct((128, 16, 128), BF),
        in_specs=[whole],
        out_specs=whole,
        compiler_params=params(),
        cost_estimate=cost(1 << 18, 1 << 20),
        name="total",
    )(mine)
    everything = lax.all_to_all(copies, ALL, split_axis=0, concat_axis=0, tiled=True)
    return everything.reshape(2048, 128)


def mask_columns(mask_plane):
    return mask_plane.astype(F32).T


def faces_kernel(state_ref, cot_ref, mask_ref, held_ref, xlo_ref, xhi_ref, ylo_ref, yhi_ref):
    p = pl.program_id(0)
    columns = mask_columns(mask_ref[0])
    for y in range(NY):
        gate = jnp.broadcast_to(columns[:, y : y + 1], (NZ, R)).astype(BF)
        held_ref[0, y] = cot_ref[0, y] * gate
    ylo_ref[0, 0] = state_ref[0, 0]
    ylo_ref[1, 0] = held_ref[0, 0]
    yhi_ref[0, 0] = state_ref[0, NY - 1]
    yhi_ref[1, 0] = held_ref[0, NY - 1]

    @pl.when(p == 0)
    def _():
        xlo_ref[0] = state_ref[0]
        xlo_ref[1] = held_ref[0]

    @pl.when(p == NX - 1)
    def _():
        xhi_ref[0] = state_ref[0]
        xhi_ref[1] = held_ref[0]


plane = pl.BlockSpec((1, NY, NZ, R), lambda p: (p, 0, 0, 0))
mask_block = pl.BlockSpec((1, NY, NZ), lambda p: (p, 0, 0))


def faces(state, cotangent, mask):
    x_face = pl.BlockSpec((2, NY, NZ, R), lambda p: (0, 0, 0, 0))
    y_face = pl.BlockSpec((2, 1, NZ, R), lambda p: (0, p, 0, 0))
    x_shape = jax.ShapeDtypeStruct((2, NY, NZ, R), BF)
    y_shape = jax.ShapeDtypeStruct((2, NX, NZ, R), BF)
    return pl.pallas_call(
        faces_kernel,
        grid=(NX,),
        out_shape=(jax.ShapeDtypeStruct((NX, NY, NZ, R), BF), x_shape, x_shape, y_shape, y_shape),
        in_specs=[plane, plane, mask_block],
        out_specs=(plane, x_face, x_face, y_face, y_face),
        compiler_params=params(),
        cost_estimate=cost(1 << 20, 9 << 20),
        name="faces",
    )(state, cotangent, mask)


def load_padded(padded, sem, centre, xlo, xhi, ylo, yhi):
    copies = [
        pltpu.make_async_copy(centre, padded.at[pl.ds(1, NX), pl.ds(1, NY)], sem.at[0]),
        pltpu.make_async_copy(xlo, padded.at[0, pl.ds(1, NY)], sem.at[1]),
        pltpu.make_async_copy(xhi, padded.at[NX + 1, pl.ds(1, NY)], sem.at[2]),
        pltpu.make_async_copy(ylo, padded.at[pl.ds(1, NX), 0], sem.at[3]),
        pltpu.make_async_copy(yhi, padded.at[pl.ds(1, NX), NY + 1], sem.at[4]),
    ]
    for copy in copies:
        copy.start()
    return copies


def build_pairs(padded, p, pairs):
    place = lax.broadcasted_iota(jnp.int32, (NZ, R), 0)

    def one_row(y, carry):
        at = pl.ds(pl.multiple_of(y * NZ, NZ), NZ)
        centre = padded[p + 1, y + 1]
        pairs[at, 0:256] = padded[p + 2, y + 1] - centre
        pairs[at, 256:512] = centre - padded[p, y + 1]
        pairs[at, 512:768] = padded[p + 1, y + 2] - centre
        pairs[at, 768:1024] = centre - padded[p + 1, y]
        wide = centre.astype(F32)
        after = jnp.where(place < NZ - 1, pltpu.roll(wide, NZ - 1, 0), 0.0)
        before = jnp.where(place > 0, pltpu.roll(wide, 1, 0), 0.0)
        pairs[at, 1024:1280] = (after - wide).astype(BF)
        pairs[at, 1280:1536] = (wide - before).astype(BF)
        return carry

    lax.fori_loop(0, NY, one_row, 0)


def inner_kernel(
    packed_ref, cot_ref, mask_ref, held_hbm, xlo_hbm, xhi_hbm, ylo_hbm, yhi_hbm,
    hi_ref, base_ref, hxlo_ref, hxhi_ref, hylo_ref, hyhi_ref, back_ref, flow_ref,
    padded, pairs, acc, sem,
):
    p = pl.program_id(0)

    @pl.when(p == 0)
    def _():
        copies = load_padded(
            padded, sem, held_hbm, xlo_hbm.at[1], xhi_hbm.at[1], ylo_hbm.at[1], yhi_hbm.at[1]
        )
        for d in range(3):
            for side in range(2):
                a, b, c, e = load_packed(packed_ref, 2 * d + side)
                sign = 1.0 - 2.0 * side
                at = (2 * d + side) * 256
                back_ref[at : at + 128, :128] = (sign * a).astype(BF)
                back_ref[at : at + 128, 128:] = (sign * b).astype(BF)
                back_ref[at + 128 : at + 256, :128] = (sign * c).astype(BF)
                back_ref[at + 128 : at + 256, 128:] = (sign * e).astype(BF)
                at = (2 * d + 1 - side) * 256
                flow_ref[at : at + 128, :128] = (-sign * a).astype(BF)
                flow_ref[at : at + 128, 128:] = (-sign * b).astype(BF)
                flow_ref[at + 128 : at + 256, :128] = (-sign * c).astype(BF)
                flow_ref[at + 128 : at + 256, 128:] = (-sign * e).astype(BF)
        for copy in copies:
            copy.wait()

    build_pairs(padded, p, pairs)
    acc[...] = jnp.dot(pairs[...], back_ref[...], preferred_element_type=F32)
    columns = mask_columns(mask_ref[0])
    for y in range(NY):
        gate = jnp.broadcast_to(columns[:, y : y + 1], (NZ, R))
        half = 0.5 * cot_ref[0, y].astype(F32)
        inner = half + (0.5 * courant) * acc[y * NZ : (y + 1) * NZ, :]
        hi_ref[0, y] = (gate * inner).astype(BF)
        base_ref[0, y] = half + inner
    hylo_ref[0] = hi_ref[0, 0]
    hyhi_ref[0] = hi_ref[0, NY - 1]

    @pl.when(p == 0)
    def _():
        hxlo_ref[...] = hi_ref[0]

    @pl.when(p == NX - 1)
    def _():
        hxhi_ref[...] = hi_ref[0]


def constant(shape):
    return pl.BlockSpec(shape, lambda p: (0,) * len(shape), pipeline_mode=pl.Buffered(1))


def kept(shape):
    return pl.BlockSpec(shape, lambda p: (0,) * len(shape))


def inner_step(packed, cotangent, mask, held, xlo, xhi, ylo, yhi):
    grid_shape = (NX, NY, NZ, R)
    x_shape = jax.ShapeDtypeStruct((NY, NZ, R), BF)
    y_shape = jax.ShapeDtypeStruct((NX, NZ, R), BF)
    y_face = pl.BlockSpec((1, NZ, R), lambda p: (p, 0, 0))
    mats = jax.ShapeDtypeStruct((1536, 256), BF)
    return pl.pallas_call(
        inner_kernel,
        grid=(NX,),
        out_shape=(
            jax.ShapeDtypeStruct(grid_shape, BF),
            jax.ShapeDtypeStruct(grid_shape, F32),
            x_shape, x_shape, y_shape, y_shape, mats, mats,
        ),
        in_specs=[constant((2048, 128)), plane, mask_block] + [raw] * 5,
        out_specs=(
            plane, plane, kept((NY, NZ, R)), kept((NY, NZ, R)), y_face, y_face,
            kept((1536, 256)), kept((1536, 256)),
        ),
        scratch_shapes=[
            pltpu.VMEM((NX + 2, NY + 2, NZ, R), BF),
            pltpu.VMEM((ROWS, 1536), BF),
            pltpu.VMEM((ROWS, R), F32),
            pltpu.SemaphoreType.DMA((5,)),
        ],
        compiler_params=params(),
        cost_estimate=cost(2 * 4096 * 256 * 1536, 14 << 20),
        name="inner",
    )(packed, cotangent, mask, held, xlo, xhi, ylo, yhi)


def middle_kernel(
    flow_ref, mask_ref, state_hbm, held_hbm, xlo_hbm, xhi_hbm, ylo_hbm, yhi_hbm,
    grads_ref, state_pad, held_pad, pairs, held_pairs, middle, acc, sem_s, sem_h,
):
    p = pl.program_id(0)

    @pl.when(p == 0)
    def _():
        first = load_padded(
            state_pad, sem_s, state_hbm, xlo_hbm.at[0], xhi_hbm.at[0], ylo_hbm.at[0], yhi_hbm.at[0]
        )
        second = load_padded(
            held_pad, sem_h, held_hbm, xlo_hbm.at[1], xhi_hbm.at[1], ylo_hbm.at[1], yhi_hbm.at[1]
        )
        grads_ref[...] = jnp.zeros_like(grads_ref)
        for copy in first + second:
            copy.wait()

    build_pairs(state_pad, p, pairs)
    acc[...] = jnp.dot(pairs[...], flow_ref[...], preferred_element_type=F32)
    columns = mask_columns(mask_ref[0])
    for y in range(NY):
        gate = jnp.broadcast_to(columns[:, y : y + 1], (NZ, R))
        flow = courant * acc[y * NZ : (y + 1) * NZ, :]
        own = state_pad[p + 1, y + 1].astype(F32)
        middle[y * NZ : (y + 1) * NZ, :] = (own + gate * flow).astype(BF)
    build_pairs(held_pad, p, held_pairs)
    grads_ref[...] += lax.dot_general(
        middle[...], held_pairs[...], (((0,), (0,)), ((), ())), preferred_element_type=F32
    )


def middle_step(flow_mats, mask, state, held, xlo, xhi, ylo, yhi):
    padded = pltpu.VMEM((NX + 2, NY + 2, NZ, R), BF)
    return pl.pallas_call(
        middle_kernel,
        grid=(NX,),
        out_shape=jax.ShapeDtypeStruct((256, 1536), F32),
        in_specs=[constant((1536, 256)), mask_block] + [raw] * 6,
        out_specs=kept((256, 1536)),
        scratch_shapes=[
            padded, padded,
            pltpu.VMEM((ROWS, 1536), BF),
            pltpu.VMEM((ROWS, 1536), BF),
            pltpu.VMEM((ROWS, R), BF),
            pltpu.VMEM((ROWS, R), F32),
            pltpu.SemaphoreType.DMA((5,)),
            pltpu.SemaphoreType.DMA((5,)),
        ],
        compiler_params=params(),
        cost_estimate=cost(4 * 4096 * 256 * 1536, 8 << 20),
        name="middle",
    )(flow_mats, mask, state, held, xlo, xhi, ylo, yhi)


def grads_kernel(
    held_grads_ref, state_ref, hi_hbm, xlo_hbm, xhi_hbm, ylo_hbm, yhi_hbm,
    out_ref, padded, pairs, acc, sem,
):
    p = pl.program_id(0)

    @pl.when(p == 0)
    def _():
        copies = load_padded(padded, sem, hi_hbm, xlo_hbm, xhi_hbm, ylo_hbm, yhi_hbm)
        acc[...] = 0.5 * held_grads_ref[...]
        for copy in copies:
            copy.wait()

    build_pairs(padded, p, pairs)
    acc[...] += lax.dot_general(
        state_ref[0].reshape(ROWS, R), pairs[...], (((0,), (0,)), ((), ())),
        preferred_element_type=F32,
    )

    @pl.when(p == NX - 1)
    def _():
        diagonals = []
        for k in range(6):
            scale = courant if k % 2 == 0 else -courant
            g = acc.at[:, pl.ds(k * 256, 256)]
            a, b, c, d = g[:128, :128], g[:128, 128:], g[128:, :128], g[128:, 128:]
            diagonals.append(
                store_packed(
                    out_ref, k, scale * (a + a.T), scale * (b + c.T), scale * (d + d.T)
                )
            )
        store_diagonals(out_ref, diagonals)


def grads_step(held_grads, state, hi, xlo, xhi, ylo, yhi):
    return pl.pallas_call(
        grads_kernel,
        grid=(NX,),
        out_shape=jax.ShapeDtypeStruct((2048, 128), BF),
        in_specs=[constant((256, 1536)), plane] + [raw] * 5,
        out_specs=kept((2048, 128)),
        scratch_shapes=[
            pltpu.VMEM((NX + 2, NY + 2, NZ, R), BF),
            pltpu.VMEM((ROWS, 1536), BF),
            pltpu.VMEM((256, 1536), F32),
            pltpu.SemaphoreType.DMA((5,)),
        ],
        compiler_params=params(),
        cost_estimate=cost(2 * 4096 * 256 * 1536, 7 << 20),
        name="grads",
    )(held_grads, state, hi, xlo, xhi, ylo, yhi)


def outer_kernel(
    back_ref, base_ref, hi_hbm, xlo_hbm, xhi_hbm, ylo_hbm, yhi_hbm,
    out_ref, padded, pairs, acc, sem,
):
    p = pl.program_id(0)

    @pl.when(p == 0)
    def _():
        copies = load_padded(padded, sem, hi_hbm, xlo_hbm, xhi_hbm, ylo_hbm, yhi_hbm)
        for copy in copies:
            copy.wait()

    build_pairs(padded, p, pairs)
    acc[...] = jnp.dot(pairs[...], back_ref[...], preferred_element_type=F32)
    for y in range(NY):
        out_ref[0, y] = (base_ref[0, y] + courant * acc[y * NZ : (y + 1) * NZ, :]).astype(BF)


def outer_step(back_mats, base, hi, xlo, xhi, ylo, yhi):
    return pl.pallas_call(
        outer_kernel,
        grid=(NX,),
        out_shape=jax.ShapeDtypeStruct((NX, NY, NZ, R), BF),
        in_specs=[constant((1536, 256)), plane] + [raw] * 5,
        out_specs=plane,
        scratch_shapes=[
            pltpu.VMEM((NX + 2, NY + 2, NZ, R), BF),
            pltpu.VMEM((ROWS, 1536), BF),
            pltpu.VMEM((ROWS, R), F32),
            pltpu.SemaphoreType.DMA((5,)),
        ],
        compiler_params=params(),
        cost_estimate=cost(2 * 4096 * 256 * 1536, 11 << 20),
        name="outer",
    )(back_mats, base, hi, xlo, xhi, ylo, yhi)


CHUNK = 512


def final_kernel(packed_ref, factors_ref, speeds_ref, signs_ref, out_ref, mats, weighted):
    @pl.when(pl.program_id(0) == 0)
    def _():
        for k in range(6):
            a, b, c, d = load_packed(packed_ref, k)
            at = k * 256
            mats[at : at + 128, :128] = a.astype(BF)
            mats[at : at + 128, 128:] = b.astype(BF)
            mats[at + 128 : at + 256, :128] = c.astype(BF)
            mats[at + 128 : at + 256, 128:] = d.astype(BF)

    rows = rate_rows(speeds_ref, signs_ref)
    columns = jnp.concatenate(rows + rows[:2], axis=0).T
    values = factors_ref[...].astype(F32)
    for k in range(6):
        rate = jnp.broadcast_to(columns[:, k : k + 1], (CHUNK, R))
        weighted[:, k * 256 : k * 256 + 256] = (rate * values).astype(BF)
    out_ref[...] = jnp.dot(weighted[...], mats[...], preferred_element_type=F32)


def final_step(packed, factors, speeds, signs):
    rows = factors.shape[0]
    return pl.pallas_call(
        final_kernel,
        grid=(rows // CHUNK,),
        out_shape=jax.ShapeDtypeStruct((rows, R), F32),
        in_specs=[
            constant((2048, 128)),
            pl.BlockSpec((CHUNK, R), lambda i: (i, 0)),
            pl.BlockSpec((3, CHUNK), lambda i: (0, i)),
            pl.BlockSpec((3, CHUNK), lambda i: (0, i)),
        ],
        out_specs=pl.BlockSpec((CHUNK, R), lambda i: (i, 0)),
        scratch_shapes=[pltpu.VMEM((1536, 256), BF), pltpu.VMEM((CHUNK, 1536), BF)],
        compiler_params=params(),
        cost_estimate=cost(2 * 2048 * 256 * 1536, 4 << 20),
        name="final",
    )(packed, factors, speeds, signs)


def exchange(lo_x, hi_x, lo_y, hi_y):
    results = []
    for axis, lo, hi in (("gx", lo_x, hi_x), (("gy", "gz"), lo_y, hi_y)):
        count = lax.axis_size(axis)
        forward = [(i, i + 1) for i in range(count - 1)]
        backward = [(i + 1, i) for i in range(count - 1)]
        results.append(lax.ppermute(hi, axis, forward))
        results.append(lax.ppermute(lo, axis, backward))
    return results


def on_device(state, cotangent, factors, speeds, signs, mask):
    packed = sum_everywhere(gram(factors, speeds, signs))
    held, xlo, xhi, ylo, yhi = faces(state, cotangent, mask)
    halos = exchange(xlo, xhi, ylo, yhi)
    hi, base, hxlo, hxhi, hylo, hyhi, back_mats, flow_mats = inner_step(
        packed, cotangent, mask, held, *halos
    )
    hi_halos = exchange(hxlo, hxhi, hylo, hyhi)
    held_grads = middle_step(flow_mats, mask, state, held, *halos)
    symmetric = sum_everywhere(grads_step(held_grads, state, hi, *hi_halos))
    grad_state = outer_step(back_mats, base, hi, *hi_halos)
    grad_factors = final_step(symmetric, factors, speeds, signs)
    return (grad_state, grad_factors)


def solution(mesh):
    placed = (
        P("gx", ("gy", "gz"), None, None),
        P("gx", ("gy", "gz"), None, None),
        P(ALL, None),
        P(None, ALL),
        P(None, ALL),
        P("gx", ("gy", "gz"), None),
    )
    return jax.shard_map(
        on_device,
        mesh=mesh,
        in_specs=placed,
        out_specs=(P("gx", ("gy", "gz"), None, None), P(ALL, None)),
        check_vma=False,
    )
```

```python
import jax
import jax.numpy as jnp
from jax import lax
from jax.experimental import pallas as pl
from jax.experimental.pallas import tpu as pltpu
from jax.sharding import PartitionSpec as P

courant = 0.2
ALL = ("gx", "gy", "gz")
BF = jnp.bfloat16
F32 = jnp.float32
NX, NY, NZ, R = 4, 8, 128, 256
ROWS = NY * NZ
whole = pl.BlockSpec(memory_space=pltpu.VMEM)
raw = pl.BlockSpec(memory_space=pl.ANY)
hbm = pl.BlockSpec(memory_space=pltpu.HBM)


def params(mib, **kw):
    return pltpu.CompilerParams(vmem_limit_bytes=mib * 1024 * 1024, **kw)


def cost(flops, bytes_accessed):
    return pl.CostEstimate(flops=flops, bytes_accessed=bytes_accessed, transcendentals=0)


def tri_masks():
    row = lax.broadcasted_iota(jnp.int32, (128, 128), 0)
    col = lax.broadcasted_iota(jnp.int32, (128, 128), 1)
    return row, col


def store_packed(out_ref, k, a, b, d):
    row, col = tri_masks()
    out_ref[k * 256 : k * 256 + 128, :] = jnp.where(row <= col, a, d).astype(BF)
    out_ref[k * 256 + 128 : k * 256 + 256, :] = b.astype(BF)
    return jnp.sum(jnp.where(row == col, d, 0.0), axis=0, keepdims=True)


def store_diagonals(out_ref, diagonals):
    zeros = jnp.zeros((10, 128), F32)
    out_ref[1536:1552, :] = jnp.concatenate(diagonals + [zeros], axis=0).astype(BF)
    out_ref[1552:2048, :] = jnp.zeros((496, 128), BF)


def load_packed(packed_ref, k):
    row, col = tri_masks()
    t = packed_ref[k * 256 : k * 256 + 128, :].astype(F32)
    b = packed_ref[k * 256 + 128 : k * 256 + 256, :].astype(F32)
    diag = packed_ref[1536:1552, :].astype(F32)[k : k + 1, :]
    tt = t.T
    a = jnp.where(row <= col, t, tt)
    d = jnp.where(row > col, t, jnp.where(row < col, tt, jnp.broadcast_to(diag, (128, 128))))
    return a, b, b.T, d


def rate_rows(speeds_ref, signs_ref):
    rows = []
    for d in range(3):
        chosen = signs_ref[d : d + 1, :].astype(F32)
        speed = speeds_ref[d : d + 1, :]
        rows.append(speed * chosen)
        rows.append(speed * (1.0 - chosen))
    return rows


def gram_kernel(factors_ref, speeds_ref, signs_ref, out_ref, turned_ref, acc_ref):
    rows = rate_rows(speeds_ref, signs_ref)
    turned = factors_ref[...].astype(F32).T
    for k in range(6):
        turned_ref[k * 256 : k * 256 + 256, :] = (turned * rows[k]).astype(BF)
    acc_ref[...] = jnp.dot(turned_ref[...], factors_ref[...], preferred_element_type=F32)
    diagonals = []
    for k in range(6):
        g = acc_ref.at[pl.ds(k * 256, 256), :]
        diagonals.append(
            store_packed(out_ref, k, g[:128, :128], g[:128, 128:], g[128:, 128:])
        )
    store_diagonals(out_ref, diagonals)


def gram(factors, speeds, signs):
    return pl.pallas_call(
        gram_kernel,
        out_shape=jax.ShapeDtypeStruct((2048, 128), BF),
        in_specs=[whole] * 3,
        out_specs=whole,
        scratch_shapes=[pltpu.VMEM((1536, 2048), BF), pltpu.VMEM((1536, 256), F32)],
        compiler_params=params(20),
        cost_estimate=cost(2 * 2048 * 256 * 1536, 2 << 20),
        name="gram",
    )(factors, speeds, signs)


def total_kernel(parts_ref, out_ref):
    total = jnp.sum(parts_ref[...].astype(F32), axis=0).astype(BF)
    out_ref[...] = jnp.broadcast_to(total[None], (128, 16, 128))


def scatter_sum(packed):
    pieces = packed.reshape(128, 16, 128)
    mine = lax.all_to_all(pieces, ALL, split_axis=0, concat_axis=0, tiled=True)
    return pl.pallas_call(
        total_kernel,
        out_shape=jax.ShapeDtypeStruct((128, 16, 128), BF),
        in_specs=[whole],
        out_specs=whole,
        compiler_params=params(4),
        cost_estimate=cost(1 << 18, 1 << 20),
        name="total",
    )(mine)


def gather(copies):
    everything = lax.all_to_all(copies, ALL, split_axis=0, concat_axis=0, tiled=True)
    return everything.reshape(2048, 128)


GRID = (NX, NY, NZ, R)
CELLS = NX * NY


def edges_kernel(
    state_hbm, cot_hbm, mask_ref, xlo_ref, xhi_ref, ylo_ref, yhi_ref, sxlo_ref, sxhi_ref, sem
):
    copies = [
        pltpu.make_async_copy(cot_hbm.at[0], xlo_ref, sem.at[0]),
        pltpu.make_async_copy(cot_hbm.at[NX - 1], xhi_ref, sem.at[1]),
        pltpu.make_async_copy(cot_hbm.at[:, 0], ylo_ref.at[1], sem.at[2]),
        pltpu.make_async_copy(cot_hbm.at[:, NY - 1], yhi_ref.at[1], sem.at[3]),
        pltpu.make_async_copy(state_hbm.at[:, 0], ylo_ref.at[0], sem.at[4]),
        pltpu.make_async_copy(state_hbm.at[:, NY - 1], yhi_ref.at[0], sem.at[5]),
        pltpu.make_async_copy(state_hbm.at[0], sxlo_ref, sem.at[6]),
        pltpu.make_async_copy(state_hbm.at[NX - 1], sxhi_ref, sem.at[7]),
    ]
    for copy in copies:
        copy.start()
    columns = mask_ref[...].reshape(CELLS, NZ).astype(F32).T

    def gate(r):
        return jnp.broadcast_to(columns[:, r : r + 1], (NZ, R)).astype(BF)

    for copy in copies:
        copy.wait()
    for y in range(NY):
        xlo_ref[y] = xlo_ref[y] * gate(y)
        xhi_ref[y] = xhi_ref[y] * gate((NX - 1) * NY + y)
    for x in range(NX):
        ylo_ref[1, x] = ylo_ref[1, x] * gate(x * NY)
        yhi_ref[1, x] = yhi_ref[1, x] * gate(x * NY + NY - 1)


x_face = jax.ShapeDtypeStruct((NY, NZ, R), BF)
y_face = jax.ShapeDtypeStruct((NX, NZ, R), BF)
y_faces = jax.ShapeDtypeStruct((2, NX, NZ, R), BF)


def edges(state, cotangent, mask):
    return pl.pallas_call(
        edges_kernel,
        out_shape=(x_face, x_face, y_faces, y_faces, x_face, x_face),
        in_specs=[hbm, hbm, whole],
        out_specs=(whole,) * 6,
        scratch_shapes=[pltpu.SemaphoreType.DMA((8,))],
        compiler_params=params(56),
        cost_estimate=cost(1 << 20, 6 << 20),
        name="edges",
    )(state, cotangent, mask)


PADDED = (NX + 2, NY + 2, NZ, R)
field_scratch = [
    pltpu.VMEM(PADDED, BF),
    pltpu.VMEM((NX + 1, ROWS, R), BF),
    pltpu.VMEM((NX, ROWS + NZ, R), BF),
    pltpu.VMEM((NX, ROWS, R), BF),
    pltpu.VMEM((NX, ROWS, R), BF),
    pltpu.SemaphoreType.DMA((NX + 4,)),
]


def start_loads(padded, sem, centre, xlo, xhi, ylo, yhi):
    inside = pl.ds(1, NY)
    planes = pl.ds(1, NX)
    pairs = [
        (xlo, padded.at[0, inside]),
        (ylo, padded.at[planes, 0]),
        (yhi, padded.at[planes, NY + 1]),
    ]
    pairs += [(centre.at[p], padded.at[p + 1, inside]) for p in range(NX)]
    pairs.append((xhi, padded.at[NX + 1, inside]))
    copies = [pltpu.make_async_copy(a, b, sem.at[i]) for i, (a, b) in enumerate(pairs)]
    for copy in copies:
        copy.start()
    return copies


def wait_all(copies):
    for copy in copies:
        copy.wait()


GROUP = 4


def at_row(y):
    return pl.ds(pl.multiple_of(y * NZ, NZ), NZ)


def build(copies, padded, dx, dy, dzp, dzm, gates=None):
    place = lax.broadcasted_iota(jnp.int32, (NZ, R), 0)
    wait_all(copies[:3])
    for p in range(NX):
        copies[3 + p].wait()

        def some_rows(n, carry, p=p):
            y0 = n * GROUP
            below = padded[p + 1, y0]
            for j in range(GROUP):
                y = y0 + j
                centre = padded[p + 1, y + 1]
                if gates is not None:
                    centre = centre * gate_of(gates, p * NY + y).astype(BF)
                    padded[p + 1, y + 1] = centre
                dx[p, at_row(y), :] = centre - padded[p, y + 1]
                dy[p, at_row(y), :] = centre - below
                below = centre
                wide = centre.astype(F32)
                minus = wide - jnp.where(place > 0, pltpu.roll(wide, 1, 0), 0.0)
                plus = jnp.where(place < NZ - 1, pltpu.roll(minus, NZ - 1, 0), -wide)
                dzm[p, at_row(y), :] = minus.astype(BF)
                dzp[p, at_row(y), :] = plus.astype(BF)
            return carry

        lax.fori_loop(0, NY // GROUP, some_rows, 0)
        dy[p, ROWS : ROWS + NZ, :] = padded[p + 1, NY + 1] - padded[p + 1, NY]
    copies[NX + 3].wait()

    def last_plane(y, carry):
        dx[NX, at_row(y), :] = padded[NX + 1, y + 1] - padded[NX, y + 1]
        return carry

    lax.fori_loop(0, NY, last_plane, 0, unroll=4)


def pieces(p, dx, dy, dzp, dzm):
    return [
        dx[p + 1], dx[p], dy[p, NZ : NZ + ROWS, :], dy[p, 0:ROWS, :], dzp[p], dzm[p],
    ]


def times(p, differences, mats_ref):
    return jnp.dot(
        jnp.concatenate(pieces(p, *differences), axis=1), mats_ref[...],
        preferred_element_type=F32,
    )


def add_products(total, left, p, differences):
    turned = left.T
    for k, piece in enumerate(pieces(p, *differences)):
        total[:, k * 256 : k * 256 + 256] += jnp.dot(turned, piece, preferred_element_type=F32)


def fill_gates(gates, mask_ref):
    columns = mask_ref[...].reshape(CELLS, NZ).astype(F32).T
    for r in range(CELLS):
        gates[r] = jnp.broadcast_to(columns[:, r : r + 1], (NZ, 128))


def gate_of(gates, r):
    gate = gates[r]
    return jnp.concatenate([gate, gate], axis=1)


def inner_kernel(
    packed_ref, mask_ref, cot_ref, xlo_hbm, xhi_hbm, ylo_hbm, yhi_hbm,
    hi_ref, base_ref, hxlo_hbm, hxhi_hbm, hylo_hbm, hyhi_hbm, back_ref, flow_ref,
    padded, dx, dy, dzp, dzm, sem, gates, out_sem,
):
    copies = start_loads(padded, sem, cot_ref, xlo_hbm, xhi_hbm, ylo_hbm.at[1], yhi_hbm.at[1])
    fill_gates(gates, mask_ref)
    for k in range(6):
        a, b, c, e = load_packed(packed_ref, k)
        sign = 1.0 if k % 2 == 0 else -1.0
        other = k + 1 - 2 * (k % 2)
        for ref, at, s in ((back_ref, k * 256, sign), (flow_ref, other * 256, -sign)):
            ref[at : at + 128, :128] = (s * a).astype(BF)
            ref[at : at + 128, 128:] = (s * b).astype(BF)
            ref[at + 128 : at + 256, :128] = (s * c).astype(BF)
            ref[at + 128 : at + 256, 128:] = (s * e).astype(BF)
    differences = (dx, dy, dzp, dzm)
    build(copies, padded, *differences, gates=gates)

    def outs(p):
        return [
            pltpu.make_async_copy(hi_ref.at[p, 0], hylo_hbm.at[p], out_sem.at[0, p]),
            pltpu.make_async_copy(hi_ref.at[p, NY - 1], hyhi_hbm.at[p], out_sem.at[1, p]),
        ]

    first = pltpu.make_async_copy(hi_ref.at[0], hxlo_hbm, out_sem.at[2, 0])
    last = pltpu.make_async_copy(hi_ref.at[NX - 1], hxhi_hbm, out_sem.at[2, 1])

    def one_plane(p, carry):
        back = times(p, differences, back_ref)
        for y in range(NY):
            half = 0.5 * cot_ref[p, y].astype(F32)
            inner = half + (0.5 * courant) * back[y * NZ : (y + 1) * NZ, :]
            hi_ref[p, y] = (gate_of(gates, p * NY + y) * inner).astype(BF)
            base_ref[p, y] = half + inner
        for copy in outs(p):
            copy.start()

        @pl.when(p == 0)
        def _():
            first.start()

        return carry

    lax.fori_loop(0, NX, one_plane, 0)
    last.start()
    for p in range(NX):
        wait_all(outs(p))
    wait_all([first, last])


def inner_step(packed, cotangent, mask, xlo, xhi, ylo, yhi):
    return pl.pallas_call(
        inner_kernel,
        out_shape=(
            pltpu.VMEM(GRID, BF), pltpu.VMEM(GRID, F32),
            x_face, x_face, y_face, y_face, pltpu.VMEM((1536, 256), BF), pltpu.VMEM((1536, 256), BF),
        ),
        in_specs=[whole, whole, whole] + [raw] * 4,
        out_specs=(whole, whole) + (hbm,) * 4 + (whole, whole),
        scratch_shapes=field_scratch
        + [pltpu.VMEM((CELLS, NZ, 128), F32), pltpu.SemaphoreType.DMA((3, NX))],
        compiler_params=params(20),
        cost_estimate=cost(2 * 4096 * 256 * 1536, 14 << 20),
        name="inner",
    )(packed, mask, cotangent, xlo, xhi, ylo, yhi)


def middle_kernel(
    flow_ref, mask_ref, state_hbm, sxlo, sxhi, cot_hbm, hxlo, hxhi, ylo, yhi,
    grads_ref, state_pad, sdx, sdy, sdzp, sdzm, sem_s, held_pad, hdx, hdy, hdzp, hdzm, sem_h,
    gates,
):
    held_copies = start_loads(held_pad, sem_h, cot_hbm, hxlo, hxhi, ylo.at[1], yhi.at[1])
    state_copies = start_loads(state_pad, sem_s, state_hbm, sxlo, sxhi, ylo.at[0], yhi.at[0])
    fill_gates(gates, mask_ref)
    grads_ref[...] = jnp.zeros_like(grads_ref)
    states, helds = (sdx, sdy, sdzp, sdzm), (hdx, hdy, hdzp, hdzm)
    build(held_copies, held_pad, *helds, gates=gates)
    build(state_copies, state_pad, *states)

    def one_plane(p, carry):
        flow = times(p, states, flow_ref)
        rows = []
        for y in range(NY):
            own = state_pad[p + 1, y + 1].astype(F32)
            moved = courant * flow[y * NZ : (y + 1) * NZ, :]
            rows.append((own + gate_of(gates, p * NY + y) * moved).astype(BF))
        for y in range(NY):
            state_pad[p + 1, y + 1] = rows[y]
        return carry

    lax.fori_loop(0, NX, one_plane, 0)

    def products(p, carry):
        middle = state_pad[p + 1, 1 : NY + 1].reshape(ROWS, R)
        add_products(grads_ref, middle, p, helds)
        return carry

    lax.fori_loop(0, NX, products, 0)


def middle_step(flow_mats, mask, state, state_x, cotangent, held_x, y_halos):
    return pl.pallas_call(
        middle_kernel,
        out_shape=pltpu.VMEM((256, 1536), F32),
        in_specs=[whole, whole, whole, raw, raw, whole] + [raw] * 4,
        out_specs=whole,
        scratch_shapes=field_scratch * 2
        + [pltpu.VMEM((CELLS, NZ, 128), F32)],
        compiler_params=params(34),
        cost_estimate=cost(4 * 4096 * 256 * 1536, 8 << 20),
        name="middle",
    )(flow_mats, mask, state, *state_x, cotangent, *held_x, *y_halos)


def last_kernel(
    held_grads_ref, state_ref, hi_ref, back_ref, base_ref, xlo_hbm, xhi_hbm, ylo_hbm, yhi_hbm,
    packed_ref, out_hbm, padded, dx, dy, dzp, dzm, sem, total, out, out_sem,
):
    copies = start_loads(padded, sem, hi_ref, xlo_hbm, xhi_hbm, ylo_hbm, yhi_hbm)
    total[...] = 0.5 * held_grads_ref[...]
    differences = (dx, dy, dzp, dzm)
    build(copies, padded, *differences)

    def out_copy(p):
        return pltpu.make_async_copy(out.at[p], out_hbm.at[p], out_sem.at[p])

    def one_plane(p, carry):
        back = times(p, differences, back_ref)
        for y in range(NY):
            out[p, y] = (base_ref[p, y] + courant * back[y * NZ : (y + 1) * NZ, :]).astype(BF)
        out_copy(p).start()
        return carry

    lax.fori_loop(0, NX, one_plane, 0)

    def products(p, carry):
        add_products(total, state_ref[p].reshape(ROWS, R), p, differences)
        return carry

    lax.fori_loop(0, NX, products, 0)
    diagonals = []
    for k in range(6):
        scale = courant if k % 2 == 0 else -courant
        g = total.at[:, pl.ds(k * 256, 256)]
        a, b, c, d = g[:128, :128], g[:128, 128:], g[128:, :128], g[128:, 128:]
        diagonals.append(
            store_packed(packed_ref, k, scale * (a + a.T), scale * (b + c.T), scale * (d + d.T))
        )
    store_diagonals(packed_ref, diagonals)
    for p in range(NX):
        out_copy(p).wait()


def last_step(held_grads, state, hi, back_mats, base, xlo, xhi, ylo, yhi):
    return pl.pallas_call(
        last_kernel,
        out_shape=(jax.ShapeDtypeStruct((2048, 128), BF), jax.ShapeDtypeStruct(GRID, BF)),
        in_specs=[whole] * 5 + [raw] * 4,
        out_specs=(whole, hbm),
        scratch_shapes=field_scratch
        + [
            pltpu.VMEM((256, 1536), F32),
            pltpu.VMEM(GRID, BF),
            pltpu.SemaphoreType.DMA((NX,)),
        ],
        compiler_params=params(24),
        cost_estimate=cost(4 * 4096 * 256 * 1536, 5 << 20),
        name="last",
    )(held_grads, state, hi, back_mats, base, xlo, xhi, ylo, yhi)


CHUNK = 512


def weighted_kernel(factors_ref, speeds_ref, signs_ref, out_ref):
    rows = rate_rows(speeds_ref, signs_ref)
    columns = jnp.concatenate(rows + rows[:2], axis=0).T
    values = factors_ref[...].astype(F32)
    for k in range(6):
        rate = jnp.broadcast_to(columns[:, k : k + 1], (CHUNK, R))
        out_ref[:, k * 256 : k * 256 + 256] = (rate * values).astype(BF)


def weigh(factors, speeds, signs):
    rows = factors.shape[0]
    return pl.pallas_call(
        weighted_kernel,
        grid=(rows // CHUNK,),
        out_shape=jax.ShapeDtypeStruct((rows, 1536), BF),
        in_specs=[
            pl.BlockSpec((CHUNK, R), lambda i: (i, 0)),
            pl.BlockSpec((3, CHUNK), lambda i: (0, i)),
            pl.BlockSpec((3, CHUNK), lambda i: (0, i)),
        ],
        out_specs=pl.BlockSpec((CHUNK, 1536), lambda i: (i, 0)),
        compiler_params=params(56),
        cost_estimate=cost(2048 * 1536, 8 << 20),
        name="weigh",
    )(factors, speeds, signs)


def final_kernel(packed_ref, weighted_ref, out_ref, mats):
    @pl.when(pl.program_id(0) == 0)
    def _():
        for k in range(6):
            a, b, c, d = load_packed(packed_ref, k)
            at = k * 256
            mats[at : at + 128, :128] = a.astype(BF)
            mats[at : at + 128, 128:] = b.astype(BF)
            mats[at + 128 : at + 256, :128] = c.astype(BF)
            mats[at + 128 : at + 256, 128:] = d.astype(BF)

    out_ref[...] = jnp.dot(weighted_ref[...], mats[...], preferred_element_type=F32)


def constant(shape):
    return pl.BlockSpec(shape, lambda i: (0,) * len(shape), pipeline_mode=pl.Buffered(1))


def final_step(packed, weighted):
    rows = weighted.shape[0]
    return pl.pallas_call(
        final_kernel,
        grid=(rows // CHUNK,),
        out_shape=jax.ShapeDtypeStruct((rows, R), F32),
        in_specs=[constant((2048, 128)), pl.BlockSpec((CHUNK, 1536), lambda i: (i, 0))],
        out_specs=pl.BlockSpec((CHUNK, R), lambda i: (i, 0)),
        scratch_shapes=[pltpu.VMEM((1536, 256), BF)],
        compiler_params=params(56),
        cost_estimate=cost(2 * 2048 * 256 * 1536, 8 << 20),
        name="final",
    )(packed, weighted)


def shift(axis, lo, hi):
    count = lax.axis_size(axis)
    forward = [(i, i + 1) for i in range(count - 1)]
    backward = [(i + 1, i) for i in range(count - 1)]
    return lax.ppermute(hi, axis, forward), lax.ppermute(lo, axis, backward)


Y_AXES = ("gy", "gz")


def near(x):
    return pltpu.with_memory_space_constraint(x, pltpu.VMEM)


def on_device(state, cotangent, factors, speeds, signs, mask):
    hxlo, hxhi, ylo, yhi, sxlo, sxhi = edges(state, cotangent, mask)
    speeds, hxlo, hxhi = lax.optimization_barrier((speeds, hxlo, hxhi))
    held_x = shift("gx", hxlo, hxhi)
    copies = scatter_sum(gram(factors, speeds, signs))
    y_halos = shift(Y_AXES, ylo, yhi)
    copies, sxlo, sxhi = lax.optimization_barrier((copies, sxlo, sxhi))
    state_x = shift("gx", sxlo, sxhi)
    packed = gather(copies)
    hi, base, hxlo, hxhi, hylo, hyhi, back_mats, flow_mats = inner_step(
        near(packed), near(cotangent), mask, *held_x, *y_halos
    )
    hi_halos = shift("gx", hxlo, hxhi) + shift(Y_AXES, hylo, hyhi)
    held_grads = middle_step(
        near(flow_mats), mask, near(state), state_x, near(cotangent), held_x, y_halos
    )
    partial, grad_state = last_step(
        near(held_grads), near(state), near(hi), near(back_mats), near(base), *hi_halos
    )
    sums = scatter_sum(partial)
    weighted = weigh(factors, speeds, signs)
    symmetric = gather(sums)
    grad_factors = final_step(symmetric, weighted)
    return (grad_state, grad_factors)


def solution(mesh):
    placed = (
        P("gx", ("gy", "gz"), None, None),
        P("gx", ("gy", "gz"), None, None),
        P(ALL, None),
        P(None, ALL),
        P(None, ALL),
        P("gx", ("gy", "gz"), None),
    )
    return jax.shard_map(
        on_device,
        mesh=mesh,
        in_specs=placed,
        out_specs=(P("gx", ("gy", "gz"), None, None), P(ALL, None)),
        check_vma=False,
    )
```

```python
import jax
import jax.numpy as jnp
from jax import lax
from jax.experimental import pallas as pl
from jax.experimental.pallas import tpu as pltpu
from jax.sharding import PartitionSpec as P

courant = 0.2
ALL = ("gx", "gy", "gz")
BF = jnp.bfloat16
F32 = jnp.float32
NX, NY, NZ, R = 4, 8, 128, 256
ROWS = NY * NZ
whole = pl.BlockSpec(memory_space=pltpu.VMEM)
raw = pl.BlockSpec(memory_space=pl.ANY)
hbm = pl.BlockSpec(memory_space=pltpu.HBM)


def params(mib, **kw):
    return pltpu.CompilerParams(vmem_limit_bytes=mib * 1024 * 1024, **kw)


def cost(flops, bytes_accessed):
    return pl.CostEstimate(flops=flops, bytes_accessed=bytes_accessed, transcendentals=0)


def tri_masks():
    row = lax.broadcasted_iota(jnp.int32, (128, 128), 0)
    col = lax.broadcasted_iota(jnp.int32, (128, 128), 1)
    return row, col


def store_packed(out_ref, k, a, b, d):
    row, col = tri_masks()
    out_ref[k * 256 : k * 256 + 128, :] = jnp.where(row <= col, a, d).astype(BF)
    out_ref[k * 256 + 128 : k * 256 + 256, :] = b.astype(BF)
    return jnp.sum(jnp.where(row == col, d, 0.0), axis=0, keepdims=True)


def store_diagonals(out_ref, diagonals):
    zeros = jnp.zeros((10, 128), F32)
    out_ref[1536:1552, :] = jnp.concatenate(diagonals + [zeros], axis=0).astype(BF)
    out_ref[1552:2048, :] = jnp.zeros((496, 128), BF)


def load_packed(packed_ref, k):
    row, col = tri_masks()
    t = packed_ref[k * 256 : k * 256 + 128, :].astype(F32)
    b = packed_ref[k * 256 + 128 : k * 256 + 256, :].astype(F32)
    diag = packed_ref[1536:1552, :].astype(F32)[k : k + 1, :]
    tt = t.T
    a = jnp.where(row <= col, t, tt)
    d = jnp.where(row > col, t, jnp.where(row < col, tt, jnp.broadcast_to(diag, (128, 128))))
    return a, b, b.T, d


def rate_rows(speeds_ref, signs_ref):
    rows = []
    for d in range(3):
        chosen = signs_ref[d : d + 1, :].astype(F32)
        speed = speeds_ref[d : d + 1, :]
        rows.append(speed * chosen)
        rows.append(speed * (1.0 - chosen))
    return rows


def gram_kernel(factors_ref, speeds_ref, signs_ref, out_ref, turned_ref, acc_ref):
    rows = rate_rows(speeds_ref, signs_ref)
    turned = factors_ref[...].astype(F32).T
    for k in range(6):
        turned_ref[k * 256 : k * 256 + 256, :] = (turned * rows[k]).astype(BF)
    acc_ref[...] = jnp.dot(turned_ref[...], factors_ref[...], preferred_element_type=F32)
    diagonals = []
    for k in range(6):
        g = acc_ref.at[pl.ds(k * 256, 256), :]
        diagonals.append(
            store_packed(out_ref, k, g[:128, :128], g[:128, 128:], g[128:, 128:])
        )
    store_diagonals(out_ref, diagonals)


def gram(factors, speeds, signs):
    return pl.pallas_call(
        gram_kernel,
        out_shape=jax.ShapeDtypeStruct((2048, 128), BF),
        in_specs=[whole] * 3,
        out_specs=whole,
        scratch_shapes=[pltpu.VMEM((1536, 2048), BF), pltpu.VMEM((1536, 256), F32)],
        compiler_params=params(20),
        cost_estimate=cost(2 * 2048 * 256 * 1536, 2 << 20),
        name="gram",
    )(factors, speeds, signs)


def total_kernel(parts_ref, out_ref):
    total = jnp.sum(parts_ref[...].astype(F32), axis=0).astype(BF)
    out_ref[...] = jnp.broadcast_to(total[None], (128, 16, 128))


def scatter_sum(packed):
    pieces = packed.reshape(128, 16, 128)
    mine = lax.all_to_all(pieces, ALL, split_axis=0, concat_axis=0, tiled=True)
    return pl.pallas_call(
        total_kernel,
        out_shape=jax.ShapeDtypeStruct((128, 16, 128), BF),
        in_specs=[whole],
        out_specs=whole,
        compiler_params=params(4),
        cost_estimate=cost(1 << 18, 1 << 20),
        name="total",
    )(mine)


def gather(copies):
    everything = lax.all_to_all(copies, ALL, split_axis=0, concat_axis=0, tiled=True)
    return everything.reshape(2048, 128)


GRID = (NX, NY, NZ, R)
CELLS = NX * NY


def edges_kernel(
    state_hbm, cot_hbm, mask_ref, xlo_ref, xhi_ref, ylo_ref, yhi_ref, sxlo_ref, sxhi_ref, sem
):
    copies = [
        pltpu.make_async_copy(cot_hbm.at[0], xlo_ref, sem.at[0]),
        pltpu.make_async_copy(cot_hbm.at[NX - 1], xhi_ref, sem.at[1]),
        pltpu.make_async_copy(cot_hbm.at[:, 0], ylo_ref.at[1], sem.at[2]),
        pltpu.make_async_copy(cot_hbm.at[:, NY - 1], yhi_ref.at[1], sem.at[3]),
        pltpu.make_async_copy(state_hbm.at[:, 0], ylo_ref.at[0], sem.at[4]),
        pltpu.make_async_copy(state_hbm.at[:, NY - 1], yhi_ref.at[0], sem.at[5]),
        pltpu.make_async_copy(state_hbm.at[0], sxlo_ref, sem.at[6]),
        pltpu.make_async_copy(state_hbm.at[NX - 1], sxhi_ref, sem.at[7]),
    ]
    for copy in copies:
        copy.start()
    columns = mask_ref[...].reshape(CELLS, NZ).astype(F32).T

    def gate(r):
        return jnp.broadcast_to(columns[:, r : r + 1], (NZ, R)).astype(BF)

    for copy in copies:
        copy.wait()
    for y in range(NY):
        xlo_ref[y] = xlo_ref[y] * gate(y)
        xhi_ref[y] = xhi_ref[y] * gate((NX - 1) * NY + y)
    for x in range(NX):
        ylo_ref[1, x] = ylo_ref[1, x] * gate(x * NY)
        yhi_ref[1, x] = yhi_ref[1, x] * gate(x * NY + NY - 1)


x_face = jax.ShapeDtypeStruct((NY, NZ, R), BF)
y_face = jax.ShapeDtypeStruct((NX, NZ, R), BF)
y_faces = jax.ShapeDtypeStruct((2, NX, NZ, R), BF)


def edges(state, cotangent, mask):
    return pl.pallas_call(
        edges_kernel,
        out_shape=(x_face, x_face, y_faces, y_faces, x_face, x_face),
        in_specs=[hbm, hbm, whole],
        out_specs=(whole,) * 6,
        scratch_shapes=[pltpu.SemaphoreType.DMA((8,))],
        compiler_params=params(56),
        cost_estimate=cost(1 << 20, 6 << 20),
        name="edges",
    )(state, cotangent, mask)


PADDED = (NX + 2, NY + 2, NZ, R)
difference_arrays = [
    pltpu.VMEM((NX + 1, ROWS, R), BF),
    pltpu.VMEM((NX, ROWS + NZ, R), BF),
    pltpu.VMEM((NX, ROWS, R), BF),
    pltpu.VMEM((NX, ROWS, R), BF),
]
load_sems = pltpu.SemaphoreType.DMA((NX + 4,))
field_scratch = [pltpu.VMEM(PADDED, BF)] + difference_arrays + [load_sems]


def start_loads(padded, sem, centre, xlo, xhi, ylo, yhi):
    inside = pl.ds(1, NY)
    planes = pl.ds(1, NX)
    pairs = [
        (xlo, padded.at[0, inside]),
        (ylo, padded.at[planes, 0]),
        (yhi, padded.at[planes, NY + 1]),
    ]
    pairs += [(centre.at[p], padded.at[p + 1, inside]) for p in range(NX)]
    pairs.append((xhi, padded.at[NX + 1, inside]))
    copies = [pltpu.make_async_copy(a, b, sem.at[i]) for i, (a, b) in enumerate(pairs)]
    for copy in copies:
        copy.start()
    return copies


def wait_all(copies):
    for copy in copies:
        copy.wait()


GROUP = 4


def at_row(y):
    return pl.ds(pl.multiple_of(y * NZ, NZ), NZ)


def build(copies, padded, dx, dy, dzp, dzm, gates=None):
    place = lax.broadcasted_iota(jnp.int32, (NZ, R), 0)
    wait_all(copies[:3])
    for p in range(NX):
        copies[3 + p].wait()

        def some_rows(n, carry, p=p):
            y0 = n * GROUP
            below = padded[p + 1, y0]
            for j in range(GROUP):
                y = y0 + j
                centre = padded[p + 1, y + 1]
                if gates is not None:
                    centre = centre * gate_of(gates, p * NY + y).astype(BF)
                    padded[p + 1, y + 1] = centre
                dx[p, at_row(y), :] = centre - padded[p, y + 1]
                dy[p, at_row(y), :] = centre - below
                below = centre
                wide = centre.astype(F32)
                minus = wide - jnp.where(place > 0, pltpu.roll(wide, 1, 0), 0.0)
                plus = jnp.where(place < NZ - 1, pltpu.roll(minus, NZ - 1, 0), -wide)
                dzm[p, at_row(y), :] = minus.astype(BF)
                dzp[p, at_row(y), :] = plus.astype(BF)
            return carry

        lax.fori_loop(0, NY // GROUP, some_rows, 0)
        dy[p, ROWS : ROWS + NZ, :] = padded[p + 1, NY + 1] - padded[p + 1, NY]
    copies[NX + 3].wait()

    def last_plane(y, carry):
        dx[NX, at_row(y), :] = padded[NX + 1, y + 1] - padded[NX, y + 1]
        return carry

    lax.fori_loop(0, NY, last_plane, 0, unroll=4)


def pieces(p, dx, dy, dzp, dzm):
    return [
        dx[p + 1], dx[p], dy[p, NZ : NZ + ROWS, :], dy[p, 0:ROWS, :], dzp[p], dzm[p],
    ]


def times(p, differences, mats_ref):
    return jnp.dot(
        jnp.concatenate(pieces(p, *differences), axis=1), mats_ref[...],
        preferred_element_type=F32,
    )


def add_products(total, left, p, differences):
    turned = left.T
    for k, piece in enumerate(pieces(p, *differences)):
        total[:, k * 256 : k * 256 + 256] += jnp.dot(turned, piece, preferred_element_type=F32)


def fill_gates(gates, mask_ref):
    columns = mask_ref[...].reshape(CELLS, NZ).astype(F32).T
    for r in range(CELLS):
        gates[r] = jnp.broadcast_to(columns[:, r : r + 1], (NZ, 128))


def gate_of(gates, r):
    gate = gates[r]
    return jnp.concatenate([gate, gate], axis=1)


def inner_kernel(
    packed_ref, mask_ref, cot_ref, xlo_hbm, xhi_hbm, ylo_hbm, yhi_hbm,
    hi_ref, base_ref, hxlo_hbm, hxhi_hbm, hylo_hbm, hyhi_hbm, back_ref, flow_ref,
    dx, dy, dzp, dzm, padded, sem, gates, out_sem,
):
    copies = start_loads(padded, sem, cot_ref, xlo_hbm, xhi_hbm, ylo_hbm.at[1], yhi_hbm.at[1])
    fill_gates(gates, mask_ref)
    for k in range(6):
        a, b, c, e = load_packed(packed_ref, k)
        sign = 1.0 if k % 2 == 0 else -1.0
        other = k + 1 - 2 * (k % 2)
        for ref, at, s in ((back_ref, k * 256, sign), (flow_ref, other * 256, -sign)):
            ref[at : at + 128, :128] = (s * a).astype(BF)
            ref[at : at + 128, 128:] = (s * b).astype(BF)
            ref[at + 128 : at + 256, :128] = (s * c).astype(BF)
            ref[at + 128 : at + 256, 128:] = (s * e).astype(BF)
    differences = (dx, dy, dzp, dzm)
    build(copies, padded, *differences, gates=gates)

    def outs(p):
        return [
            pltpu.make_async_copy(hi_ref.at[p, 0], hylo_hbm.at[p], out_sem.at[0, p]),
            pltpu.make_async_copy(hi_ref.at[p, NY - 1], hyhi_hbm.at[p], out_sem.at[1, p]),
        ]

    first = pltpu.make_async_copy(hi_ref.at[0], hxlo_hbm, out_sem.at[2, 0])
    last = pltpu.make_async_copy(hi_ref.at[NX - 1], hxhi_hbm, out_sem.at[2, 1])

    def one_plane(p, carry):
        back = times(p, differences, back_ref)
        for y in range(NY):
            half = 0.5 * cot_ref[p, y].astype(F32)
            inner = half + (0.5 * courant) * back[y * NZ : (y + 1) * NZ, :]
            hi_ref[p, y] = (gate_of(gates, p * NY + y) * inner).astype(BF)
            base_ref[p, y] = half + inner
        for copy in outs(p):
            copy.start()

        @pl.when(p == 0)
        def _():
            first.start()

        return carry

    lax.fori_loop(0, NX, one_plane, 0)
    last.start()
    for p in range(NX):
        wait_all(outs(p))
    wait_all([first, last])


def inner_step(packed, cotangent, mask, xlo, xhi, ylo, yhi):
    return pl.pallas_call(
        inner_kernel,
        out_shape=(
            pltpu.VMEM(GRID, BF), pltpu.VMEM(GRID, F32),
            x_face, x_face, y_face, y_face, pltpu.VMEM((1536, 256), BF), pltpu.VMEM((1536, 256), BF),
        ) + tuple(difference_arrays),
        in_specs=[whole, whole, whole] + [raw] * 4,
        out_specs=(whole, whole) + (hbm,) * 4 + (whole,) * 6,
        scratch_shapes=[
            pltpu.VMEM(PADDED, BF),
            load_sems,
            pltpu.VMEM((CELLS, NZ, 128), F32),
            pltpu.SemaphoreType.DMA((3, NX)),
        ],
        compiler_params=params(20),
        cost_estimate=cost(2 * 4096 * 256 * 1536, 14 << 20),
        name="inner",
    )(packed, mask, cotangent, xlo, xhi, ylo, yhi)


def middle_kernel(
    flow_ref, mask_ref, state_ref, sxlo, sxhi, ylo, yhi, hdx, hdy, hdzp, hdzm,
    grads_ref, state_pad, sdx, sdy, sdzp, sdzm, sem_s, gates,
):
    state_copies = start_loads(state_pad, sem_s, state_ref, sxlo, sxhi, ylo.at[0], yhi.at[0])
    fill_gates(gates, mask_ref)
    grads_ref[...] = jnp.zeros_like(grads_ref)
    states, helds = (sdx, sdy, sdzp, sdzm), (hdx, hdy, hdzp, hdzm)
    build(state_copies, state_pad, *states)

    def one_plane(p, carry):
        flow = times(p, states, flow_ref)
        rows = []
        for y in range(NY):
            own = state_pad[p + 1, y + 1].astype(F32)
            moved = courant * flow[y * NZ : (y + 1) * NZ, :]
            rows.append((own + gate_of(gates, p * NY + y) * moved).astype(BF))
        for y in range(NY):
            state_pad[p + 1, y + 1] = rows[y]
        return carry

    lax.fori_loop(0, NX, one_plane, 0)

    def products(p, carry):
        middle = state_pad[p + 1, 1 : NY + 1].reshape(ROWS, R)
        add_products(grads_ref, middle, p, helds)
        return carry

    lax.fori_loop(0, NX, products, 0)


def middle_step(flow_mats, mask, state, state_x, y_halos, held_differences):
    return pl.pallas_call(
        middle_kernel,
        out_shape=pltpu.VMEM((256, 1536), F32),
        in_specs=[whole] * 3 + [raw] * 4 + [whole] * 4,
        out_specs=whole,
        scratch_shapes=field_scratch + [pltpu.VMEM((CELLS, NZ, 128), F32)],
        compiler_params=params(22),
        cost_estimate=cost(4 * 4096 * 256 * 1536, 4 << 20),
        name="middle",
    )(flow_mats, mask, state, *state_x, *y_halos, *held_differences)


def last_kernel(
    held_grads_ref, state_ref, hi_ref, back_ref, base_ref, xlo_hbm, xhi_hbm, ylo_hbm, yhi_hbm,
    packed_ref, out_hbm, padded, dx, dy, dzp, dzm, sem, total, out, out_sem,
):
    copies = start_loads(padded, sem, hi_ref, xlo_hbm, xhi_hbm, ylo_hbm, yhi_hbm)
    total[...] = 0.5 * held_grads_ref[...]
    differences = (dx, dy, dzp, dzm)
    build(copies, padded, *differences)

    def out_copy(p):
        return pltpu.make_async_copy(out.at[p], out_hbm.at[p], out_sem.at[p])

    def one_plane(p, carry):
        back = times(p, differences, back_ref)
        for y in range(NY):
            out[p, y] = (base_ref[p, y] + courant * back[y * NZ : (y + 1) * NZ, :]).astype(BF)
        out_copy(p).start()
        return carry

    lax.fori_loop(0, NX, one_plane, 0)

    def products(p, carry):
        add_products(total, state_ref[p].reshape(ROWS, R), p, differences)
        return carry

    lax.fori_loop(0, NX, products, 0)
    diagonals = []
    for k in range(6):
        scale = courant if k % 2 == 0 else -courant
        g = total.at[:, pl.ds(k * 256, 256)]
        a, b, c, d = g[:128, :128], g[:128, 128:], g[128:, :128], g[128:, 128:]
        diagonals.append(
            store_packed(packed_ref, k, scale * (a + a.T), scale * (b + c.T), scale * (d + d.T))
        )
    store_diagonals(packed_ref, diagonals)
    for p in range(NX):
        out_copy(p).wait()


def last_step(held_grads, state, hi, back_mats, base, xlo, xhi, ylo, yhi):
    return pl.pallas_call(
        last_kernel,
        out_shape=(jax.ShapeDtypeStruct((2048, 128), BF), jax.ShapeDtypeStruct(GRID, BF)),
        in_specs=[whole] * 5 + [raw] * 4,
        out_specs=(whole, hbm),
        scratch_shapes=field_scratch
        + [
            pltpu.VMEM((256, 1536), F32),
            pltpu.VMEM(GRID, BF),
            pltpu.SemaphoreType.DMA((NX,)),
        ],
        compiler_params=params(24),
        cost_estimate=cost(4 * 4096 * 256 * 1536, 5 << 20),
        name="last",
    )(held_grads, state, hi, back_mats, base, xlo, xhi, ylo, yhi)


CHUNK = 512


def weighted_kernel(factors_ref, speeds_ref, signs_ref, out_ref):
    rows = rate_rows(speeds_ref, signs_ref)
    columns = jnp.concatenate(rows + rows[:2], axis=0).T
    values = factors_ref[...].astype(F32)
    for k in range(6):
        rate = jnp.broadcast_to(columns[:, k : k + 1], (CHUNK, R))
        out_ref[:, k * 256 : k * 256 + 256] = (rate * values).astype(BF)


def weigh(factors, speeds, signs):
    rows = factors.shape[0]
    return pl.pallas_call(
        weighted_kernel,
        grid=(rows // CHUNK,),
        out_shape=jax.ShapeDtypeStruct((rows, 1536), BF),
        in_specs=[
            pl.BlockSpec((CHUNK, R), lambda i: (i, 0)),
            pl.BlockSpec((3, CHUNK), lambda i: (0, i)),
            pl.BlockSpec((3, CHUNK), lambda i: (0, i)),
        ],
        out_specs=pl.BlockSpec((CHUNK, 1536), lambda i: (i, 0)),
        compiler_params=params(56),
        cost_estimate=cost(2048 * 1536, 8 << 20),
        name="weigh",
    )(factors, speeds, signs)


def final_kernel(packed_ref, weighted_hbm, out_hbm, mats, weighted, out, sem, out_sem):
    chunks = weighted.shape[0] // CHUNK
    loads, stores = [], []
    for i in range(chunks):
        at = pl.ds(i * CHUNK, CHUNK)
        loads.append(pltpu.make_async_copy(weighted_hbm.at[at], weighted.at[at], sem.at[i]))
        stores.append(pltpu.make_async_copy(out.at[at], out_hbm.at[at], out_sem.at[i]))
        loads[-1].start()
    for k in range(6):
        a, b, c, d = load_packed(packed_ref, k)
        at = k * 256
        mats[at : at + 128, :128] = a.astype(BF)
        mats[at : at + 128, 128:] = b.astype(BF)
        mats[at + 128 : at + 256, :128] = c.astype(BF)
        mats[at + 128 : at + 256, 128:] = d.astype(BF)
    for i in range(chunks):
        rows = slice(i * CHUNK, (i + 1) * CHUNK)
        loads[i].wait()
        out[rows, :] = jnp.dot(weighted[rows, :], mats[...], preferred_element_type=F32)
        stores[i].start()
    for store in stores:
        store.wait()


def final_step(packed, weighted):
    rows = weighted.shape[0]
    return pl.pallas_call(
        final_kernel,
        out_shape=jax.ShapeDtypeStruct((rows, R), F32),
        in_specs=[whole, hbm],
        out_specs=hbm,
        scratch_shapes=[
            pltpu.VMEM((1536, 256), BF),
            pltpu.VMEM((rows, 1536), BF),
            pltpu.VMEM((rows, R), F32),
            pltpu.SemaphoreType.DMA((rows // CHUNK,)),
            pltpu.SemaphoreType.DMA((rows // CHUNK,)),
        ],
        compiler_params=params(56),
        cost_estimate=cost(2 * 2048 * 256 * 1536, 8 << 20),
        name="final",
    )(packed, weighted)


def shift(axis, lo, hi):
    count = lax.axis_size(axis)
    forward = [(i, i + 1) for i in range(count - 1)]
    backward = [(i + 1, i) for i in range(count - 1)]
    return lax.ppermute(hi, axis, forward), lax.ppermute(lo, axis, backward)


Y_AXES = ("gy", "gz")


def near(x):
    return pltpu.with_memory_space_constraint(x, pltpu.VMEM)


def on_device(state, cotangent, factors, speeds, signs, mask):
    hxlo, hxhi, ylo, yhi, sxlo, sxhi = edges(state, cotangent, mask)
    speeds, hxlo, hxhi = lax.optimization_barrier((speeds, hxlo, hxhi))
    held_x = shift("gx", hxlo, hxhi)
    packed = gram(factors, speeds, signs)
    copies = scatter_sum(packed)
    y_halos = shift(Y_AXES, ylo, yhi)
    copies, sxlo, sxhi = lax.optimization_barrier((copies, sxlo, sxhi))
    state_x = shift("gx", sxlo, sxhi)
    packed = gather(copies)
    hi, base, hxlo, hxhi, hylo, hyhi, back_mats, flow_mats, *held_differences = inner_step(
        near(packed), near(cotangent), mask, *held_x, *y_halos
    )
    hi_halos = shift("gx", hxlo, hxhi) + shift(Y_AXES, hylo, hyhi)
    held_grads = middle_step(
        near(flow_mats), mask, near(state), state_x, y_halos, [near(d) for d in held_differences]
    )
    partial, grad_state = last_step(
        near(held_grads), near(state), near(hi), near(back_mats), near(base), *hi_halos
    )
    sums = scatter_sum(partial)
    weighted = weigh(factors, speeds, signs)
    symmetric = gather(sums)
    grad_factors = final_step(symmetric, weighted)
    return (grad_state, grad_factors)


def solution(mesh):
    placed = (
        P("gx", ("gy", "gz"), None, None),
        P("gx", ("gy", "gz"), None, None),
        P(ALL, None),
        P(None, ALL),
        P(None, ALL),
        P("gx", ("gy", "gz"), None),
    )
    return jax.shard_map(
        on_device,
        mesh=mesh,
        in_specs=placed,
        out_specs=(P("gx", ("gy", "gz"), None, None), P(ALL, None)),
        check_vma=False,
    )
```

```python
import jax
import jax.numpy as jnp
from jax import lax
from jax.experimental import pallas as pl
from jax.experimental.pallas import tpu as pltpu
from jax.sharding import PartitionSpec as P

courant = 0.2
ALL = ("gx", "gy", "gz")
BF = jnp.bfloat16
F32 = jnp.float32
NX, NY, NZ, R = 4, 8, 128, 256
ROWS = NY * NZ
whole = pl.BlockSpec(memory_space=pltpu.VMEM)
raw = pl.BlockSpec(memory_space=pl.ANY)
hbm = pl.BlockSpec(memory_space=pltpu.HBM)


def params(mib, **kw):
    return pltpu.CompilerParams(vmem_limit_bytes=mib * 1024 * 1024, **kw)


def cost(flops, bytes_accessed):
    return pl.CostEstimate(flops=flops, bytes_accessed=bytes_accessed, transcendentals=0)


def tri_masks():
    row = lax.broadcasted_iota(jnp.int32, (128, 128), 0)
    col = lax.broadcasted_iota(jnp.int32, (128, 128), 1)
    return row, col


def store_packed(out_ref, k, a, b, d):
    row, col = tri_masks()
    out_ref[k * 256 : k * 256 + 128, :] = jnp.where(row <= col, a, d).astype(BF)
    out_ref[k * 256 + 128 : k * 256 + 256, :] = b.astype(BF)
    return jnp.sum(jnp.where(row == col, d, 0.0), axis=0, keepdims=True)


def store_diagonals(out_ref, diagonals):
    zeros = jnp.zeros((10, 128), F32)
    out_ref[1536:1552, :] = jnp.concatenate(diagonals + [zeros], axis=0).astype(BF)
    out_ref[1552:2048, :] = jnp.zeros((496, 128), BF)


def load_packed(packed_ref, k):
    row, col = tri_masks()
    t = packed_ref[k * 256 : k * 256 + 128, :].astype(F32)
    b = packed_ref[k * 256 + 128 : k * 256 + 256, :].astype(F32)
    diag = packed_ref[1536:1552, :].astype(F32)[k : k + 1, :]
    tt = t.T
    a = jnp.where(row <= col, t, tt)
    d = jnp.where(row > col, t, jnp.where(row < col, tt, jnp.broadcast_to(diag, (128, 128))))
    return a, b, b.T, d


def rate_rows(speeds_ref, signs_ref):
    rows = []
    for d in range(3):
        chosen = signs_ref[d : d + 1, :].astype(F32)
        speed = speeds_ref[d : d + 1, :]
        rows.append(speed * chosen)
        rows.append(speed * (1.0 - chosen))
    return rows


def gram_kernel(factors_ref, speeds_ref, signs_ref, out_ref, turned_ref, acc_ref):
    rows = rate_rows(speeds_ref, signs_ref)
    turned = factors_ref[...].astype(F32).T
    for k in range(6):
        turned_ref[k * 256 : k * 256 + 256, :] = (turned * rows[k]).astype(BF)
    acc_ref[...] = jnp.dot(turned_ref[...], factors_ref[...], preferred_element_type=F32)
    diagonals = []
    for k in range(6):
        g = acc_ref.at[pl.ds(k * 256, 256), :]
        diagonals.append(
            store_packed(out_ref, k, g[:128, :128], g[:128, 128:], g[128:, 128:])
        )
    store_diagonals(out_ref, diagonals)


def gram(factors, speeds, signs):
    return pl.pallas_call(
        gram_kernel,
        out_shape=jax.ShapeDtypeStruct((2048, 128), BF),
        in_specs=[whole] * 3,
        out_specs=whole,
        scratch_shapes=[pltpu.VMEM((1536, 2048), BF), pltpu.VMEM((1536, 256), F32)],
        compiler_params=params(20),
        cost_estimate=cost(2 * 2048 * 256 * 1536, 2 << 20),
        name="gram",
    )(factors, speeds, signs)


def total_kernel(parts_ref, out_ref):
    total = jnp.sum(parts_ref[...].astype(F32), axis=0).astype(BF)
    out_ref[...] = jnp.broadcast_to(total[None], (128, 16, 128))


def scatter_sum(packed):
    pieces = packed.reshape(128, 16, 128)
    mine = lax.all_to_all(pieces, ALL, split_axis=0, concat_axis=0, tiled=True)
    return pl.pallas_call(
        total_kernel,
        out_shape=jax.ShapeDtypeStruct((128, 16, 128), BF),
        in_specs=[whole],
        out_specs=whole,
        compiler_params=params(4),
        cost_estimate=cost(1 << 18, 1 << 20),
        name="total",
    )(mine)


def gather(copies):
    everything = lax.all_to_all(copies, ALL, split_axis=0, concat_axis=0, tiled=True)
    return everything.reshape(2048, 128)


GRID = (NX, NY, NZ, R)
CELLS = NX * NY


def edges_kernel(
    state_hbm, cot_hbm, mask_ref, xlo_ref, xhi_ref, ylo_ref, yhi_ref, sxlo_ref, sxhi_ref, sem
):
    copies = [
        pltpu.make_async_copy(cot_hbm.at[0], xlo_ref, sem.at[0]),
        pltpu.make_async_copy(cot_hbm.at[NX - 1], xhi_ref, sem.at[1]),
        pltpu.make_async_copy(cot_hbm.at[:, 0], ylo_ref.at[1], sem.at[2]),
        pltpu.make_async_copy(cot_hbm.at[:, NY - 1], yhi_ref.at[1], sem.at[3]),
        pltpu.make_async_copy(state_hbm.at[:, 0], ylo_ref.at[0], sem.at[4]),
        pltpu.make_async_copy(state_hbm.at[:, NY - 1], yhi_ref.at[0], sem.at[5]),
        pltpu.make_async_copy(state_hbm.at[0], sxlo_ref, sem.at[6]),
        pltpu.make_async_copy(state_hbm.at[NX - 1], sxhi_ref, sem.at[7]),
    ]
    for copy in copies:
        copy.start()
    columns = mask_ref[...].reshape(CELLS, NZ).astype(F32).T

    def gate(r):
        return jnp.broadcast_to(columns[:, r : r + 1], (NZ, R)).astype(BF)

    for copy in copies:
        copy.wait()
    for y in range(NY):
        xlo_ref[y] = xlo_ref[y] * gate(y)
        xhi_ref[y] = xhi_ref[y] * gate((NX - 1) * NY + y)
    for x in range(NX):
        ylo_ref[1, x] = ylo_ref[1, x] * gate(x * NY)
        yhi_ref[1, x] = yhi_ref[1, x] * gate(x * NY + NY - 1)


x_face = jax.ShapeDtypeStruct((NY, NZ, R), BF)
y_face = jax.ShapeDtypeStruct((NX, NZ, R), BF)
y_faces = jax.ShapeDtypeStruct((2, NX, NZ, R), BF)


def edges(state, cotangent, mask):
    return pl.pallas_call(
        edges_kernel,
        out_shape=(x_face, x_face, y_faces, y_faces, x_face, x_face),
        in_specs=[hbm, hbm, whole],
        out_specs=(whole,) * 6,
        scratch_shapes=[pltpu.SemaphoreType.DMA((8,))],
        compiler_params=params(56),
        cost_estimate=cost(1 << 20, 6 << 20),
        name="edges",
    )(state, cotangent, mask)


PADDED = (NX + 2, NY + 2, NZ, R)
difference_arrays = [
    pltpu.VMEM((NX + 1, ROWS, R), BF),
    pltpu.VMEM((NX, ROWS + NZ, R), BF),
    pltpu.VMEM((NX, ROWS, R), BF),
    pltpu.VMEM((NX, ROWS, R), BF),
]
load_sems = pltpu.SemaphoreType.DMA((NX + 4,))
field_scratch = [pltpu.VMEM(PADDED, BF)] + difference_arrays + [load_sems]


def start_loads(padded, sem, centre, xlo, xhi, ylo, yhi):
    inside = pl.ds(1, NY)
    planes = pl.ds(1, NX)
    pairs = [
        (xlo, padded.at[0, inside]),
        (ylo, padded.at[planes, 0]),
        (yhi, padded.at[planes, NY + 1]),
    ]
    pairs += [(centre.at[p], padded.at[p + 1, inside]) for p in range(NX)]
    pairs.append((xhi, padded.at[NX + 1, inside]))
    copies = [pltpu.make_async_copy(a, b, sem.at[i]) for i, (a, b) in enumerate(pairs)]
    for copy in copies:
        copy.start()
    return copies


def wait_all(copies):
    for copy in copies:
        copy.wait()


GROUP = 4


def at_row(y):
    return pl.ds(pl.multiple_of(y * NZ, NZ), NZ)


def build(copies, padded, dx, dy, dzp, dzm, gates=None):
    place = lax.broadcasted_iota(jnp.int32, (NZ, R), 0)
    wait_all(copies[:3])
    for p in range(NX):
        copies[3 + p].wait()

        def some_rows(n, carry, p=p):
            y0 = n * GROUP
            below = padded[p + 1, y0]
            for j in range(GROUP):
                y = y0 + j
                centre = padded[p + 1, y + 1]
                if gates is not None:
                    centre = centre * gate_of(gates, p * NY + y).astype(BF)
                    padded[p + 1, y + 1] = centre
                dx[p, at_row(y), :] = centre - padded[p, y + 1]
                dy[p, at_row(y), :] = centre - below
                below = centre
                wide = centre.astype(F32)
                minus = wide - jnp.where(place > 0, pltpu.roll(wide, 1, 0), 0.0)
                plus = jnp.where(place < NZ - 1, pltpu.roll(minus, NZ - 1, 0), -wide)
                dzm[p, at_row(y), :] = minus.astype(BF)
                dzp[p, at_row(y), :] = plus.astype(BF)
            return carry

        lax.fori_loop(0, NY // GROUP, some_rows, 0)
        dy[p, ROWS : ROWS + NZ, :] = padded[p + 1, NY + 1] - padded[p + 1, NY]
    copies[NX + 3].wait()

    def last_plane(y, carry):
        dx[NX, at_row(y), :] = padded[NX + 1, y + 1] - padded[NX, y + 1]
        return carry

    lax.fori_loop(0, NY, last_plane, 0, unroll=4)


def pieces(p, dx, dy, dzp, dzm):
    return [
        dx[p + 1], dx[p], dy[p, NZ : NZ + ROWS, :], dy[p, 0:ROWS, :], dzp[p], dzm[p],
    ]


def times(p, differences, mats_ref):
    return jnp.dot(
        jnp.concatenate(pieces(p, *differences), axis=1), mats_ref[...],
        preferred_element_type=F32,
    )


def add_products(total, left, p, differences):
    turned = left.T
    for k, piece in enumerate(pieces(p, *differences)):
        total[:, k * 256 : k * 256 + 256] += jnp.dot(turned, piece, preferred_element_type=F32)


def fill_gates(gates, mask_ref):
    columns = mask_ref[...].reshape(CELLS, NZ).astype(F32).T
    for r in range(CELLS):
        gates[r] = jnp.broadcast_to(columns[:, r : r + 1], (NZ, 128))


def gate_of(gates, r):
    gate = gates[r]
    return jnp.concatenate([gate, gate], axis=1)


def inner_kernel(
    packed_ref, mask_ref, cot_ref, xlo_hbm, xhi_hbm, ylo_hbm, yhi_hbm,
    hi_ref, base_ref, hxlo_hbm, hxhi_hbm, hylo_hbm, hyhi_hbm, back_ref, flow_ref,
    dx, dy, dzp, dzm, padded, sem, gates, out_sem,
):
    copies = start_loads(padded, sem, cot_ref, xlo_hbm, xhi_hbm, ylo_hbm.at[1], yhi_hbm.at[1])
    fill_gates(gates, mask_ref)
    for k in range(6):
        a, b, c, e = load_packed(packed_ref, k)
        sign = 1.0 if k % 2 == 0 else -1.0
        other = k + 1 - 2 * (k % 2)
        for ref, at, s in ((back_ref, k * 256, sign), (flow_ref, other * 256, -sign)):
            ref[at : at + 128, :128] = (s * a).astype(BF)
            ref[at : at + 128, 128:] = (s * b).astype(BF)
            ref[at + 128 : at + 256, :128] = (s * c).astype(BF)
            ref[at + 128 : at + 256, 128:] = (s * e).astype(BF)
    differences = (dx, dy, dzp, dzm)
    build(copies, padded, *differences, gates=gates)

    def outs(p):
        return [
            pltpu.make_async_copy(hi_ref.at[p, 0], hylo_hbm.at[p], out_sem.at[0, p]),
            pltpu.make_async_copy(hi_ref.at[p, NY - 1], hyhi_hbm.at[p], out_sem.at[1, p]),
        ]

    first = pltpu.make_async_copy(hi_ref.at[0], hxlo_hbm, out_sem.at[2, 0])
    last = pltpu.make_async_copy(hi_ref.at[NX - 1], hxhi_hbm, out_sem.at[2, 1])

    def one_plane(p, carry):
        back = times(p, differences, back_ref)
        for y in range(NY):
            half = 0.5 * cot_ref[p, y].astype(F32)
            inner = half + (0.5 * courant) * back[y * NZ : (y + 1) * NZ, :]
            hi_ref[p, y] = (gate_of(gates, p * NY + y) * inner).astype(BF)
            base_ref[p, y] = half + inner
        for copy in outs(p):
            copy.start()

        @pl.when(p == 0)
        def _():
            first.start()

        return carry

    lax.fori_loop(0, NX, one_plane, 0)
    last.start()
    for p in range(NX):
        wait_all(outs(p))
    wait_all([first, last])


def inner_step(packed, cotangent, mask, xlo, xhi, ylo, yhi):
    return pl.pallas_call(
        inner_kernel,
        out_shape=(
            pltpu.VMEM(GRID, BF), pltpu.VMEM(GRID, F32),
            x_face, x_face, y_face, y_face, pltpu.VMEM((1536, 256), BF), pltpu.VMEM((1536, 256), BF),
        ) + tuple(difference_arrays),
        in_specs=[whole, whole, whole] + [raw] * 4,
        out_specs=(whole, whole) + (hbm,) * 4 + (whole,) * 6,
        scratch_shapes=[
            pltpu.VMEM(PADDED, BF),
            load_sems,
            pltpu.VMEM((CELLS, NZ, 128), F32),
            pltpu.SemaphoreType.DMA((3, NX)),
        ],
        compiler_params=params(20),
        cost_estimate=cost(2 * 4096 * 256 * 1536, 14 << 20),
        name="inner",
    )(packed, mask, cotangent, xlo, xhi, ylo, yhi)


def middle_kernel(
    flow_ref, mask_ref, state_ref, sxlo, sxhi, ylo, yhi, hdx, hdy, hdzp, hdzm,
    grads_ref, state_pad, sdx, sdy, sdzp, sdzm, sem_s, gates,
):
    state_copies = start_loads(state_pad, sem_s, state_ref, sxlo, sxhi, ylo.at[0], yhi.at[0])
    fill_gates(gates, mask_ref)
    grads_ref[...] = jnp.zeros_like(grads_ref)
    states, helds = (sdx, sdy, sdzp, sdzm), (hdx, hdy, hdzp, hdzm)
    build(state_copies, state_pad, *states)

    def one_plane(p, carry):
        flow = times(p, states, flow_ref)
        rows = []
        for y in range(NY):
            own = state_pad[p + 1, y + 1].astype(F32)
            moved = courant * flow[y * NZ : (y + 1) * NZ, :]
            rows.append((own + gate_of(gates, p * NY + y) * moved).astype(BF))
        for y in range(NY):
            state_pad[p + 1, y + 1] = rows[y]
        return carry

    lax.fori_loop(0, NX, one_plane, 0)

    def products(p, carry):
        middle = state_pad[p + 1, 1 : NY + 1].reshape(ROWS, R)
        add_products(grads_ref, middle, p, helds)
        return carry

    lax.fori_loop(0, NX, products, 0)


def middle_step(flow_mats, mask, state, state_x, y_halos, held_differences):
    return pl.pallas_call(
        middle_kernel,
        out_shape=pltpu.VMEM((256, 1536), F32),
        in_specs=[whole] * 3 + [raw] * 4 + [whole] * 4,
        out_specs=whole,
        scratch_shapes=field_scratch + [pltpu.VMEM((CELLS, NZ, 128), F32)],
        compiler_params=params(22),
        cost_estimate=cost(4 * 4096 * 256 * 1536, 4 << 20),
        name="middle",
    )(flow_mats, mask, state, *state_x, *y_halos, *held_differences)


def last_kernel(
    held_grads_ref, state_ref, hi_ref, back_ref, base_ref, xlo_hbm, xhi_hbm, ylo_hbm, yhi_hbm,
    packed_ref, out_hbm, padded, dx, dy, dzp, dzm, sem, total, out, out_sem,
):
    copies = start_loads(padded, sem, hi_ref, xlo_hbm, xhi_hbm, ylo_hbm, yhi_hbm)
    total[...] = 0.5 * held_grads_ref[...]
    differences = (dx, dy, dzp, dzm)
    build(copies, padded, *differences)

    def out_copy(p):
        return pltpu.make_async_copy(out.at[p], out_hbm.at[p], out_sem.at[p])

    def one_plane(p, carry):
        back = times(p, differences, back_ref)
        for y in range(NY):
            out[p, y] = (base_ref[p, y] + courant * back[y * NZ : (y + 1) * NZ, :]).astype(BF)
        out_copy(p).start()
        return carry

    lax.fori_loop(0, NX, one_plane, 0)

    def products(p, carry):
        add_products(total, state_ref[p].reshape(ROWS, R), p, differences)
        return carry

    lax.fori_loop(0, NX, products, 0)
    diagonals = []
    for k in range(6):
        scale = courant if k % 2 == 0 else -courant
        g = total.at[:, pl.ds(k * 256, 256)]
        a, b, c, d = g[:128, :128], g[:128, 128:], g[128:, :128], g[128:, 128:]
        diagonals.append(
            store_packed(packed_ref, k, scale * (a + a.T), scale * (b + c.T), scale * (d + d.T))
        )
    store_diagonals(packed_ref, diagonals)
    for p in range(NX):
        out_copy(p).wait()


def last_step(held_grads, state, hi, back_mats, base, xlo, xhi, ylo, yhi):
    return pl.pallas_call(
        last_kernel,
        out_shape=(jax.ShapeDtypeStruct((2048, 128), BF), jax.ShapeDtypeStruct(GRID, BF)),
        in_specs=[whole] * 5 + [raw] * 4,
        out_specs=(whole, hbm),
        scratch_shapes=field_scratch
        + [
            pltpu.VMEM((256, 1536), F32),
            pltpu.VMEM(GRID, BF),
            pltpu.SemaphoreType.DMA((NX,)),
        ],
        compiler_params=params(24),
        cost_estimate=cost(4 * 4096 * 256 * 1536, 5 << 20),
        name="last",
    )(held_grads, state, hi, back_mats, base, xlo, xhi, ylo, yhi)


CHUNK = 512


def weighted_kernel(factors_ref, speeds_ref, signs_ref, out_ref):
    rows = rate_rows(speeds_ref, signs_ref)
    columns = jnp.concatenate(rows + rows[:2], axis=0).T
    values = factors_ref[...].astype(F32)
    for k in range(6):
        rate = jnp.broadcast_to(columns[:, k : k + 1], (CHUNK, R))
        out_ref[:, k * 256 : k * 256 + 256] = (rate * values).astype(BF)


def weigh(factors, speeds, signs):
    rows = factors.shape[0]
    return pl.pallas_call(
        weighted_kernel,
        grid=(rows // CHUNK,),
        out_shape=jax.ShapeDtypeStruct((rows, 1536), BF),
        in_specs=[
            pl.BlockSpec((CHUNK, R), lambda i: (i, 0)),
            pl.BlockSpec((3, CHUNK), lambda i: (0, i)),
            pl.BlockSpec((3, CHUNK), lambda i: (0, i)),
        ],
        out_specs=pl.BlockSpec((CHUNK, 1536), lambda i: (i, 0)),
        compiler_params=params(56),
        cost_estimate=cost(2048 * 1536, 8 << 20),
        name="weigh",
    )(factors, speeds, signs)


def final_kernel(packed_ref, weighted_ref, out_ref, mats):
    @pl.when(pl.program_id(0) == 0)
    def _():
        for k in range(6):
            a, b, c, d = load_packed(packed_ref, k)
            at = k * 256
            mats[at : at + 128, :128] = a.astype(BF)
            mats[at : at + 128, 128:] = b.astype(BF)
            mats[at + 128 : at + 256, :128] = c.astype(BF)
            mats[at + 128 : at + 256, 128:] = d.astype(BF)

    out_ref[...] = jnp.dot(weighted_ref[...], mats[...], preferred_element_type=F32)


def constant(shape):
    return pl.BlockSpec(shape, lambda i: (0,) * len(shape), pipeline_mode=pl.Buffered(1))


def final_step(packed, weighted):
    rows = weighted.shape[0]
    return pl.pallas_call(
        final_kernel,
        grid=(rows // CHUNK,),
        out_shape=jax.ShapeDtypeStruct((rows, R), F32),
        in_specs=[constant((2048, 128)), pl.BlockSpec((CHUNK, 1536), lambda i: (i, 0))],
        out_specs=pl.BlockSpec((CHUNK, R), lambda i: (i, 0)),
        scratch_shapes=[pltpu.VMEM((1536, 256), BF)],
        compiler_params=params(56),
        cost_estimate=cost(2 * 2048 * 256 * 1536, 8 << 20),
        name="final",
    )(packed, weighted)


def shift(axis, lo, hi):
    count = lax.axis_size(axis)
    forward = [(i, i + 1) for i in range(count - 1)]
    backward = [(i + 1, i) for i in range(count - 1)]
    from_below = lax.ppermute(hi, axis, forward)
    from_above = lax.ppermute(lo, axis, backward)
    return from_below, from_above


Y_AXES = ("gy", "gz")


def near(x):
    return pltpu.with_memory_space_constraint(x, pltpu.VMEM)


def on_device(state, cotangent, factors, speeds, signs, mask):
    hxlo, hxhi, ylo, yhi, sxlo, sxhi = edges(state, cotangent, mask)
    speeds, hxlo, hxhi = lax.optimization_barrier((speeds, hxlo, hxhi))
    held_x = shift("gx", hxlo, hxhi)
    copies = scatter_sum(gram(factors, speeds, signs))
    y_halos = shift(Y_AXES, ylo, yhi)
    copies, sxlo, sxhi = lax.optimization_barrier((copies, sxlo, sxhi))
    state_x = shift("gx", sxlo, sxhi)
    packed = gather(copies)
    hi, base, hxlo, hxhi, hylo, hyhi, back_mats, flow_mats, *held_differences = inner_step(
        near(packed), near(cotangent), mask, *held_x, *y_halos
    )
    hi_halos = shift("gx", hxlo, hxhi) + shift(Y_AXES, hylo, hyhi)
    held_grads = middle_step(
        near(flow_mats), mask, near(state), state_x, y_halos, [near(d) for d in held_differences]
    )
    partial, grad_state = last_step(
        near(held_grads), near(state), near(hi), near(back_mats), near(base), *hi_halos
    )
    sums = scatter_sum(partial)
    weighted = weigh(factors, speeds, signs)
    symmetric = gather(sums)
    grad_factors = final_step(symmetric, weighted)
    return (grad_state, grad_factors)


def solution(mesh):
    placed = (
        P("gx", ("gy", "gz"), None, None),
        P("gx", ("gy", "gz"), None, None),
        P(ALL, None),
        P(None, ALL),
        P(None, ALL),
        P("gx", ("gy", "gz"), None),
    )

    return jax.shard_map(
        on_device,
        mesh=mesh,
        in_specs=placed,
        out_specs=(P("gx", ("gy", "gz"), None, None), P(ALL, None)),
        check_vma=False,
    )
```

```python
import jax
import jax.numpy as jnp
from jax import lax
from jax.experimental import pallas as pl
from jax.experimental.pallas import tpu as pltpu
from jax.sharding import PartitionSpec as P

courant = 0.2
ALL = ("gx", "gy", "gz")
BF = jnp.bfloat16
F32 = jnp.float32
NX, NY, NZ, R = 4, 8, 128, 256
ROWS = NY * NZ
whole = pl.BlockSpec(memory_space=pltpu.VMEM)
raw = pl.BlockSpec(memory_space=pl.ANY)
hbm = pl.BlockSpec(memory_space=pltpu.HBM)


def params(mib, **kw):
    return pltpu.CompilerParams(vmem_limit_bytes=mib * 1024 * 1024, **kw)


def cost(flops, bytes_accessed):
    return pl.CostEstimate(flops=flops, bytes_accessed=bytes_accessed, transcendentals=0)


def tri_masks():
    row = lax.broadcasted_iota(jnp.int32, (128, 128), 0)
    col = lax.broadcasted_iota(jnp.int32, (128, 128), 1)
    return row, col


def store_packed(out_ref, k, a, b, d):
    row, col = tri_masks()
    out_ref[k * 256 : k * 256 + 128, :] = jnp.where(row <= col, a, d).astype(BF)
    out_ref[k * 256 + 128 : k * 256 + 256, :] = b.astype(BF)
    return jnp.sum(jnp.where(row == col, d, 0.0), axis=0, keepdims=True)


def store_diagonals(out_ref, diagonals):
    zeros = jnp.zeros((10, 128), F32)
    out_ref[1536:1552, :] = jnp.concatenate(diagonals + [zeros], axis=0).astype(BF)
    out_ref[1552:2048, :] = jnp.zeros((496, 128), BF)


def load_packed(packed_ref, k):
    row, col = tri_masks()
    t = packed_ref[k * 256 : k * 256 + 128, :].astype(F32)
    b = packed_ref[k * 256 + 128 : k * 256 + 256, :].astype(F32)
    diag = packed_ref[1536:1552, :].astype(F32)[k : k + 1, :]
    tt = t.T
    a = jnp.where(row <= col, t, tt)
    d = jnp.where(row > col, t, jnp.where(row < col, tt, jnp.broadcast_to(diag, (128, 128))))
    return a, b, b.T, d


def rate_rows(speeds_ref, signs_ref):
    rows = []
    for d in range(3):
        chosen = signs_ref[d : d + 1, :].astype(F32)
        speed = speeds_ref[d : d + 1, :]
        rows.append(speed * chosen)
        rows.append(speed * (1.0 - chosen))
    return rows


def gram_kernel(factors_ref, speeds_ref, signs_ref, out_ref, turned_ref, acc_ref):
    rows = rate_rows(speeds_ref, signs_ref)
    turned = factors_ref[...].astype(F32).T
    for k in range(6):
        turned_ref[k * 256 : k * 256 + 256, :] = (turned * rows[k]).astype(BF)
    acc_ref[...] = jnp.dot(turned_ref[...], factors_ref[...], preferred_element_type=F32)
    diagonals = []
    for k in range(6):
        g = acc_ref.at[pl.ds(k * 256, 256), :]
        diagonals.append(
            store_packed(out_ref, k, g[:128, :128], g[:128, 128:], g[128:, 128:])
        )
    store_diagonals(out_ref, diagonals)


def gram(factors, speeds, signs):
    return pl.pallas_call(
        gram_kernel,
        out_shape=jax.ShapeDtypeStruct((2048, 128), BF),
        in_specs=[whole] * 3,
        out_specs=whole,
        scratch_shapes=[pltpu.VMEM((1536, 2048), BF), pltpu.VMEM((1536, 256), F32)],
        compiler_params=params(20),
        cost_estimate=cost(2 * 2048 * 256 * 1536, 2 << 20),
        name="gram",
    )(factors, speeds, signs)


def total_kernel(parts_ref, out_ref):
    total = jnp.sum(parts_ref[...].astype(F32), axis=0).astype(BF)
    out_ref[...] = jnp.broadcast_to(total[None], (128, 16, 128))


def scatter_sum(packed):
    pieces = packed.reshape(128, 16, 128)
    mine = lax.all_to_all(pieces, ALL, split_axis=0, concat_axis=0, tiled=True)
    return pl.pallas_call(
        total_kernel,
        out_shape=jax.ShapeDtypeStruct((128, 16, 128), BF),
        in_specs=[whole],
        out_specs=whole,
        compiler_params=params(4),
        cost_estimate=cost(1 << 18, 1 << 20),
        name="total",
    )(mine)


def gather(copies):
    everything = lax.all_to_all(copies, ALL, split_axis=0, concat_axis=0, tiled=True)
    return everything.reshape(2048, 128)


GRID = (NX, NY, NZ, R)
CELLS = NX * NY


def mask_gate(mask_ref):
    columns = mask_ref[...].reshape(CELLS, NZ).astype(F32).T
    return lambda r: jnp.broadcast_to(columns[:, r : r + 1], (NZ, R)).astype(BF)


def held_x_kernel(cot_hbm, mask_ref, xlo_hbm, xhi_hbm, xlo, xhi, sem, out_sem):
    ins = [
        pltpu.make_async_copy(cot_hbm.at[0], xlo, sem.at[0]),
        pltpu.make_async_copy(cot_hbm.at[NX - 1], xhi, sem.at[1]),
    ]
    outs = [
        pltpu.make_async_copy(xlo, xlo_hbm, out_sem.at[0]),
        pltpu.make_async_copy(xhi, xhi_hbm, out_sem.at[1]),
    ]
    for copy in ins:
        copy.start()
    gate = mask_gate(mask_ref)
    for i, face in enumerate((xlo, xhi)):
        ins[i].wait()
        for y in range(NY):
            face[y] = face[y] * gate(i * (NX - 1) * NY + y)
        outs[i].start()
    for copy in outs:
        copy.wait()


def other_faces_kernel(
    state_hbm, cot_hbm, mask_ref, ylo_hbm, yhi_hbm, sxlo_hbm, sxhi_hbm,
    ylo, yhi, sxlo, sxhi, sem, out_sem,
):
    ins, outs = [], []
    for i, (y, face) in enumerate(((0, ylo), (NY - 1, yhi))):
        ins.append(pltpu.make_async_copy(cot_hbm.at[:, y], face.at[1], sem.at[2 * i]))
        ins.append(pltpu.make_async_copy(state_hbm.at[:, y], face.at[0], sem.at[2 * i + 1]))
        outs.append(pltpu.make_async_copy(face, (ylo_hbm, yhi_hbm)[i], out_sem.at[i]))
    for i, (x, face) in enumerate(((0, sxlo), (NX - 1, sxhi))):
        ins.append(pltpu.make_async_copy(state_hbm.at[x], face, sem.at[4 + i]))
        outs.append(pltpu.make_async_copy(face, (sxlo_hbm, sxhi_hbm)[i], out_sem.at[2 + i]))
    for copy in ins:
        copy.start()
    gate = mask_gate(mask_ref)
    for i, face in enumerate((ylo, yhi)):
        ins[2 * i].wait()
        ins[2 * i + 1].wait()
        for x in range(NX):
            face[1, x] = face[1, x] * gate(x * NY + i * (NY - 1))
        outs[i].start()
    for i in range(2):
        ins[4 + i].wait()
        outs[2 + i].start()
    for copy in outs:
        copy.wait()


x_face = jax.ShapeDtypeStruct((NY, NZ, R), BF)
y_face = jax.ShapeDtypeStruct((NX, NZ, R), BF)
two_y_faces = jax.ShapeDtypeStruct((2, NX, NZ, R), BF)


def held_x_faces(cotangent, mask):
    face = pltpu.VMEM((NY, NZ, R), BF)
    sems = pltpu.SemaphoreType.DMA((2,))
    return pl.pallas_call(
        held_x_kernel,
        out_shape=(x_face, x_face),
        in_specs=[hbm, whole],
        out_specs=(hbm, hbm),
        scratch_shapes=[face, face, sems, sems],
        compiler_params=params(56),
        cost_estimate=cost(1 << 20, 2 << 20),
        name="held_x_faces",
    )(cotangent, mask)


def other_faces(state, cotangent, mask):
    x, y = pltpu.VMEM((NY, NZ, R), BF), pltpu.VMEM((2, NX, NZ, R), BF)
    return pl.pallas_call(
        other_faces_kernel,
        out_shape=(two_y_faces, two_y_faces, x_face, x_face),
        in_specs=[hbm, hbm, whole],
        out_specs=(hbm,) * 4,
        scratch_shapes=[
            y, y, x, x, pltpu.SemaphoreType.DMA((6,)), pltpu.SemaphoreType.DMA((4,)),
        ],
        compiler_params=params(56),
        cost_estimate=cost(1 << 20, 4 << 20),
        name="other_faces",
    )(state, cotangent, mask)


PADDED = (NX + 2, NY + 2, NZ, R)
difference_arrays = [
    pltpu.VMEM((NX + 1, ROWS, R), BF),
    pltpu.VMEM((NX, ROWS + NZ, R), BF),
    pltpu.VMEM((NX, ROWS, R), BF),
    pltpu.VMEM((NX, ROWS, R), BF),
]
load_sems = pltpu.SemaphoreType.DMA((NX + 4,))
field_scratch = [pltpu.VMEM(PADDED, BF)] + difference_arrays + [load_sems]


def start_loads(padded, sem, centre, xlo, xhi, ylo, yhi):
    inside = pl.ds(1, NY)
    planes = pl.ds(1, NX)
    pairs = [
        (xlo, padded.at[0, inside]),
        (ylo, padded.at[planes, 0]),
        (yhi, padded.at[planes, NY + 1]),
    ]
    pairs += [(centre.at[p], padded.at[p + 1, inside]) for p in range(NX)]
    pairs.append((xhi, padded.at[NX + 1, inside]))
    copies = [pltpu.make_async_copy(a, b, sem.at[i]) for i, (a, b) in enumerate(pairs)]
    for copy in copies:
        copy.start()
    return copies


def wait_all(copies):
    for copy in copies:
        copy.wait()


GROUP = 4


def at_row(y):
    return pl.ds(pl.multiple_of(y * NZ, NZ), NZ)


def build(copies, padded, dx, dy, dzp, dzm, gates=None):
    place = lax.broadcasted_iota(jnp.int32, (NZ, R), 0)
    wait_all(copies[:3])
    for p in range(NX):
        copies[3 + p].wait()

        def some_rows(n, carry, p=p):
            y0 = n * GROUP
            below = padded[p + 1, y0]
            for j in range(GROUP):
                y = y0 + j
                centre = padded[p + 1, y + 1]
                if gates is not None:
                    centre = centre * gate_of(gates, p * NY + y).astype(BF)
                    padded[p + 1, y + 1] = centre
                dx[p, at_row(y), :] = centre - padded[p, y + 1]
                dy[p, at_row(y), :] = centre - below
                below = centre
                wide = centre.astype(F32)
                minus = wide - jnp.where(place > 0, pltpu.roll(wide, 1, 0), 0.0)
                plus = jnp.where(place < NZ - 1, pltpu.roll(minus, NZ - 1, 0), -wide)
                dzm[p, at_row(y), :] = minus.astype(BF)
                dzp[p, at_row(y), :] = plus.astype(BF)
            return carry

        lax.fori_loop(0, NY // GROUP, some_rows, 0)
        dy[p, ROWS : ROWS + NZ, :] = padded[p + 1, NY + 1] - padded[p + 1, NY]
    copies[NX + 3].wait()

    def last_plane(y, carry):
        dx[NX, at_row(y), :] = padded[NX + 1, y + 1] - padded[NX, y + 1]
        return carry

    lax.fori_loop(0, NY, last_plane, 0, unroll=4)


def pieces(p, dx, dy, dzp, dzm):
    return [
        dx[p + 1], dx[p], dy[p, NZ : NZ + ROWS, :], dy[p, 0:ROWS, :], dzp[p], dzm[p],
    ]


def times(p, differences, mats_ref):
    return jnp.dot(
        jnp.concatenate(pieces(p, *differences), axis=1), mats_ref[...],
        preferred_element_type=F32,
    )


def add_products(total, left, p, differences):
    turned = left.T
    for k, piece in enumerate(pieces(p, *differences)):
        total[:, k * 256 : k * 256 + 256] += jnp.dot(turned, piece, preferred_element_type=F32)


def fill_gates(gates, mask_ref):
    columns = mask_ref[...].reshape(CELLS, NZ).astype(F32).T
    for r in range(CELLS):
        gates[r] = jnp.broadcast_to(columns[:, r : r + 1], (NZ, 128))


def gate_of(gates, r):
    gate = gates[r]
    return jnp.concatenate([gate, gate], axis=1)


def inner_kernel(
    packed_ref, mask_ref, cot_ref, xlo_hbm, xhi_hbm, ylo_hbm, yhi_hbm,
    hi_ref, base_ref, hxlo_hbm, hxhi_hbm, hylo_hbm, hyhi_hbm, back_ref, flow_ref,
    dx, dy, dzp, dzm, padded, sem, gates, out_sem,
):
    copies = start_loads(padded, sem, cot_ref, xlo_hbm, xhi_hbm, ylo_hbm.at[1], yhi_hbm.at[1])
    fill_gates(gates, mask_ref)
    for k in range(6):
        a, b, c, e = load_packed(packed_ref, k)
        sign = 1.0 if k % 2 == 0 else -1.0
        other = k + 1 - 2 * (k % 2)
        for ref, at, s in ((back_ref, k * 256, sign), (flow_ref, other * 256, -sign)):
            ref[at : at + 128, :128] = (s * a).astype(BF)
            ref[at : at + 128, 128:] = (s * b).astype(BF)
            ref[at + 128 : at + 256, :128] = (s * c).astype(BF)
            ref[at + 128 : at + 256, 128:] = (s * e).astype(BF)
    differences = (dx, dy, dzp, dzm)
    build(copies, padded, *differences, gates=gates)

    def outs(p):
        return [
            pltpu.make_async_copy(hi_ref.at[p, 0], hylo_hbm.at[p], out_sem.at[0, p]),
            pltpu.make_async_copy(hi_ref.at[p, NY - 1], hyhi_hbm.at[p], out_sem.at[1, p]),
        ]

    first = pltpu.make_async_copy(hi_ref.at[0], hxlo_hbm, out_sem.at[2, 0])
    last = pltpu.make_async_copy(hi_ref.at[NX - 1], hxhi_hbm, out_sem.at[2, 1])

    def one_plane(p, carry):
        back = times(p, differences, back_ref)
        for y in range(NY):
            half = 0.5 * cot_ref[p, y].astype(F32)
            inner = half + (0.5 * courant) * back[y * NZ : (y + 1) * NZ, :]
            hi_ref[p, y] = (gate_of(gates, p * NY + y) * inner).astype(BF)
            base_ref[p, y] = half + inner
        for copy in outs(p):
            copy.start()

        @pl.when(p == 0)
        def _():
            first.start()

        return carry

    lax.fori_loop(0, NX, one_plane, 0)
    last.start()
    for p in range(NX):
        wait_all(outs(p))
    wait_all([first, last])


def inner_step(packed, cotangent, mask, xlo, xhi, ylo, yhi):
    return pl.pallas_call(
        inner_kernel,
        out_shape=(
            pltpu.VMEM(GRID, BF), pltpu.VMEM(GRID, F32),
            x_face, x_face, y_face, y_face, pltpu.VMEM((1536, 256), BF), pltpu.VMEM((1536, 256), BF),
        ) + tuple(difference_arrays),
        in_specs=[whole, whole, whole] + [raw] * 4,
        out_specs=(whole, whole) + (hbm,) * 4 + (whole,) * 6,
        scratch_shapes=[
            pltpu.VMEM(PADDED, BF),
            load_sems,
            pltpu.VMEM((CELLS, NZ, 128), F32),
            pltpu.SemaphoreType.DMA((3, NX)),
        ],
        compiler_params=params(20),
        cost_estimate=cost(2 * 4096 * 256 * 1536, 14 << 20),
        name="inner",
    )(packed, mask, cotangent, xlo, xhi, ylo, yhi)


def middle_kernel(
    flow_ref, mask_ref, state_ref, sxlo, sxhi, ylo, yhi, hdx, hdy, hdzp, hdzm,
    grads_ref, state_pad, sdx, sdy, sdzp, sdzm, sem_s, gates,
):
    state_copies = start_loads(state_pad, sem_s, state_ref, sxlo, sxhi, ylo.at[0], yhi.at[0])
    fill_gates(gates, mask_ref)
    grads_ref[...] = jnp.zeros_like(grads_ref)
    states, helds = (sdx, sdy, sdzp, sdzm), (hdx, hdy, hdzp, hdzm)
    build(state_copies, state_pad, *states)

    def one_plane(p, carry):
        flow = times(p, states, flow_ref)
        rows = []
        for y in range(NY):
            own = state_pad[p + 1, y + 1].astype(F32)
            moved = courant * flow[y * NZ : (y + 1) * NZ, :]
            rows.append((own + gate_of(gates, p * NY + y) * moved).astype(BF))
        for y in range(NY):
            state_pad[p + 1, y + 1] = rows[y]
        return carry

    lax.fori_loop(0, NX, one_plane, 0)

    def products(p, carry):
        middle = state_pad[p + 1, 1 : NY + 1].reshape(ROWS, R)
        add_products(grads_ref, middle, p, helds)
        return carry

    lax.fori_loop(0, NX, products, 0)


def middle_step(flow_mats, mask, state, state_x, y_halos, held_differences):
    return pl.pallas_call(
        middle_kernel,
        out_shape=pltpu.VMEM((256, 1536), F32),
        in_specs=[whole] * 3 + [raw] * 4 + [whole] * 4,
        out_specs=whole,
        scratch_shapes=field_scratch + [pltpu.VMEM((CELLS, NZ, 128), F32)],
        compiler_params=params(22),
        cost_estimate=cost(4 * 4096 * 256 * 1536, 4 << 20),
        name="middle",
    )(flow_mats, mask, state, *state_x, *y_halos, *held_differences)


def last_kernel(
    held_grads_ref, state_ref, hi_ref, back_ref, base_ref, xlo_hbm, xhi_hbm, ylo_hbm, yhi_hbm,
    packed_ref, out_hbm, padded, dx, dy, dzp, dzm, sem, total, out, out_sem,
):
    copies = start_loads(padded, sem, hi_ref, xlo_hbm, xhi_hbm, ylo_hbm, yhi_hbm)
    total[...] = 0.5 * held_grads_ref[...]
    differences = (dx, dy, dzp, dzm)
    build(copies, padded, *differences)

    def out_copy(p):
        return pltpu.make_async_copy(out.at[p], out_hbm.at[p], out_sem.at[p])

    def one_plane(p, carry):
        back = times(p, differences, back_ref)
        for y in range(NY):
            out[p, y] = (base_ref[p, y] + courant * back[y * NZ : (y + 1) * NZ, :]).astype(BF)
        out_copy(p).start()
        return carry

    lax.fori_loop(0, NX, one_plane, 0)

    def products(p, carry):
        add_products(total, state_ref[p].reshape(ROWS, R), p, differences)
        return carry

    lax.fori_loop(0, NX, products, 0)
    diagonals = []
    for k in range(6):
        scale = courant if k % 2 == 0 else -courant
        g = total.at[:, pl.ds(k * 256, 256)]
        a, b, c, d = g[:128, :128], g[:128, 128:], g[128:, :128], g[128:, 128:]
        diagonals.append(
            store_packed(packed_ref, k, scale * (a + a.T), scale * (b + c.T), scale * (d + d.T))
        )
    store_diagonals(packed_ref, diagonals)
    for p in range(NX):
        out_copy(p).wait()


def last_step(held_grads, state, hi, back_mats, base, xlo, xhi, ylo, yhi):
    return pl.pallas_call(
        last_kernel,
        out_shape=(jax.ShapeDtypeStruct((2048, 128), BF), jax.ShapeDtypeStruct(GRID, BF)),
        in_specs=[whole] * 5 + [raw] * 4,
        out_specs=(whole, hbm),
        scratch_shapes=field_scratch
        + [
            pltpu.VMEM((256, 1536), F32),
            pltpu.VMEM(GRID, BF),
            pltpu.SemaphoreType.DMA((NX,)),
        ],
        compiler_params=params(24),
        cost_estimate=cost(4 * 4096 * 256 * 1536, 5 << 20),
        name="last",
    )(held_grads, state, hi, back_mats, base, xlo, xhi, ylo, yhi)


CHUNK = 512


def weighted_kernel(factors_ref, speeds_ref, signs_ref, out_ref):
    rows = rate_rows(speeds_ref, signs_ref)
    columns = jnp.concatenate(rows + rows[:2], axis=0).T
    values = factors_ref[...].astype(F32)
    for k in range(6):
        rate = jnp.broadcast_to(columns[:, k : k + 1], (CHUNK, R))
        out_ref[:, k * 256 : k * 256 + 256] = (rate * values).astype(BF)


def weigh(factors, speeds, signs):
    rows = factors.shape[0]
    return pl.pallas_call(
        weighted_kernel,
        grid=(rows // CHUNK,),
        out_shape=jax.ShapeDtypeStruct((rows, 1536), BF),
        in_specs=[
            pl.BlockSpec((CHUNK, R), lambda i: (i, 0)),
            pl.BlockSpec((3, CHUNK), lambda i: (0, i)),
            pl.BlockSpec((3, CHUNK), lambda i: (0, i)),
        ],
        out_specs=pl.BlockSpec((CHUNK, 1536), lambda i: (i, 0)),
        compiler_params=params(56),
        cost_estimate=cost(2048 * 1536, 8 << 20),
        name="weigh",
    )(factors, speeds, signs)


def final_kernel(packed_ref, weighted_ref, out_ref, mats):
    @pl.when(pl.program_id(0) == 0)
    def _():
        for k in range(6):
            a, b, c, d = load_packed(packed_ref, k)
            at = k * 256
            mats[at : at + 128, :128] = a.astype(BF)
            mats[at : at + 128, 128:] = b.astype(BF)
            mats[at + 128 : at + 256, :128] = c.astype(BF)
            mats[at + 128 : at + 256, 128:] = d.astype(BF)

    out_ref[...] = jnp.dot(weighted_ref[...], mats[...], preferred_element_type=F32)


def constant(shape):
    return pl.BlockSpec(shape, lambda i: (0,) * len(shape), pipeline_mode=pl.Buffered(1))


def final_step(packed, weighted):
    rows = weighted.shape[0]
    return pl.pallas_call(
        final_kernel,
        grid=(rows // CHUNK,),
        out_shape=jax.ShapeDtypeStruct((rows, R), F32),
        in_specs=[constant((2048, 128)), pl.BlockSpec((CHUNK, 1536), lambda i: (i, 0))],
        out_specs=pl.BlockSpec((CHUNK, R), lambda i: (i, 0)),
        scratch_shapes=[pltpu.VMEM((1536, 256), BF)],
        compiler_params=params(58),
        cost_estimate=cost(2 * 2048 * 256 * 1536, 8 << 20),
        name="final",
    )(packed, weighted)


def shift(axis, lo, hi):
    count = lax.axis_size(axis)
    forward = [(i, i + 1) for i in range(count - 1)]
    backward = [(i + 1, i) for i in range(count - 1)]
    from_below = lax.ppermute(hi, axis, forward)
    from_above = lax.ppermute(lo, axis, backward)
    return from_below, from_above


Y_AXES = ("gy", "gz")


def near(x):
    return pltpu.with_memory_space_constraint(x, pltpu.VMEM)


def on_device(state, cotangent, factors, speeds, signs, mask):
    hxlo, hxhi = held_x_faces(cotangent, mask)
    held_x = shift("gx", hxlo, hxhi)
    copies = scatter_sum(gram(factors, speeds, signs))
    ylo, yhi, sxlo, sxhi = other_faces(state, cotangent, mask)
    y_halos = shift(Y_AXES, ylo, yhi)
    copies, sxlo, sxhi = lax.optimization_barrier((copies, sxlo, sxhi))
    state_x = shift("gx", sxlo, sxhi)
    packed = gather(copies)
    hi, base, hxlo, hxhi, hylo, hyhi, back_mats, flow_mats, *held_differences = inner_step(
        near(packed), near(cotangent), mask, *held_x, *y_halos
    )
    hi_halos = shift("gx", hxlo, hxhi) + shift(Y_AXES, hylo, hyhi)
    held_grads = middle_step(
        near(flow_mats), mask, near(state), state_x, y_halos, [near(d) for d in held_differences]
    )
    partial, grad_state = last_step(
        near(held_grads), near(state), near(hi), near(back_mats), near(base), *hi_halos
    )
    sums = scatter_sum(partial)
    weighted = weigh(factors, speeds, signs)
    symmetric = gather(sums)
    grad_factors = final_step(near(symmetric), weighted)
    return (grad_state, grad_factors)


def solution(mesh):
    placed = (
        P("gx", ("gy", "gz"), None, None),
        P("gx", ("gy", "gz"), None, None),
        P(ALL, None),
        P(None, ALL),
        P(None, ALL),
        P("gx", ("gy", "gz"), None),
    )

    return jax.shard_map(
        on_device,
        mesh=mesh,
        in_specs=placed,
        out_specs=(P("gx", ("gy", "gz"), None, None), P(ALL, None)),
        check_vma=False,
    )
```

```python
import jax
import jax.numpy as jnp
from jax import lax
from jax.experimental import pallas as pl
from jax.experimental.pallas import tpu as pltpu
from jax.sharding import PartitionSpec as P

courant = 0.2
ALL = ("gx", "gy", "gz")
BF = jnp.bfloat16
F32 = jnp.float32
NX, NY, NZ, R = 4, 8, 128, 256
ROWS = NY * NZ
whole = pl.BlockSpec(memory_space=pltpu.VMEM)
raw = pl.BlockSpec(memory_space=pl.ANY)
hbm = pl.BlockSpec(memory_space=pltpu.HBM)


def params(mib, **kw):
    return pltpu.CompilerParams(vmem_limit_bytes=mib * 1024 * 1024, **kw)


def cost(flops, bytes_accessed):
    return pl.CostEstimate(flops=flops, bytes_accessed=bytes_accessed, transcendentals=0)


def tri_masks():
    row = lax.broadcasted_iota(jnp.int32, (128, 128), 0)
    col = lax.broadcasted_iota(jnp.int32, (128, 128), 1)
    return row, col


def store_packed(out_ref, k, a, b, d):
    row, col = tri_masks()
    out_ref[k * 256 : k * 256 + 128, :] = jnp.where(row <= col, a, d).astype(BF)
    out_ref[k * 256 + 128 : k * 256 + 256, :] = b.astype(BF)
    return jnp.sum(jnp.where(row == col, d, 0.0), axis=0, keepdims=True)


def store_diagonals(out_ref, diagonals):
    zeros = jnp.zeros((10, 128), F32)
    out_ref[1536:1552, :] = jnp.concatenate(diagonals + [zeros], axis=0).astype(BF)
    out_ref[1552:2048, :] = jnp.zeros((496, 128), BF)


def load_packed(packed_ref, k):
    row, col = tri_masks()
    t = packed_ref[k * 256 : k * 256 + 128, :].astype(F32)
    b = packed_ref[k * 256 + 128 : k * 256 + 256, :].astype(F32)
    diag = packed_ref[1536:1552, :].astype(F32)[k : k + 1, :]
    tt = t.T
    a = jnp.where(row <= col, t, tt)
    d = jnp.where(row > col, t, jnp.where(row < col, tt, jnp.broadcast_to(diag, (128, 128))))
    return a, b, b.T, d


def rate_rows(speeds_ref, signs_ref):
    rows = []
    for d in range(3):
        chosen = signs_ref[d : d + 1, :].astype(F32)
        speed = speeds_ref[d : d + 1, :]
        rows.append(speed * chosen)
        rows.append(speed * (1.0 - chosen))
    return rows


def gram_kernel(factors_ref, speeds_ref, signs_ref, out_ref, turned_ref, acc_ref):
    rows = rate_rows(speeds_ref, signs_ref)
    turned = factors_ref[...].astype(F32).T
    for k in range(6):
        turned_ref[k * 256 : k * 256 + 256, :] = (turned * rows[k]).astype(BF)
    acc_ref[...] = jnp.dot(turned_ref[...], factors_ref[...], preferred_element_type=F32)
    diagonals = []
    for k in range(6):
        g = acc_ref.at[pl.ds(k * 256, 256), :]
        diagonals.append(
            store_packed(out_ref, k, g[:128, :128], g[:128, 128:], g[128:, 128:])
        )
    store_diagonals(out_ref, diagonals)


def gram(factors, speeds, signs):
    return pl.pallas_call(
        gram_kernel,
        out_shape=jax.ShapeDtypeStruct((2048, 128), BF),
        in_specs=[whole] * 3,
        out_specs=whole,
        scratch_shapes=[pltpu.VMEM((1536, 2048), BF), pltpu.VMEM((1536, 256), F32)],
        compiler_params=params(20),
        cost_estimate=cost(2 * 2048 * 256 * 1536, 2 << 20),
        name="gram",
    )(factors, speeds, signs)


def total_kernel(parts_ref, out_ref):
    total = jnp.sum(parts_ref[...].astype(F32), axis=0).astype(BF)
    out_ref[...] = jnp.broadcast_to(total[None], (128, 16, 128))


def scatter_sum(packed):
    pieces = packed.reshape(128, 16, 128)
    mine = lax.all_to_all(pieces, ALL, split_axis=0, concat_axis=0, tiled=True)
    return pl.pallas_call(
        total_kernel,
        out_shape=jax.ShapeDtypeStruct((128, 16, 128), BF),
        in_specs=[whole],
        out_specs=whole,
        compiler_params=params(4),
        cost_estimate=cost(1 << 18, 1 << 20),
        name="total",
    )(mine)


def gather(copies):
    everything = lax.all_to_all(copies, ALL, split_axis=0, concat_axis=0, tiled=True)
    return everything.reshape(2048, 128)


GRID = (NX, NY, NZ, R)
CELLS = NX * NY


def mask_gate(mask_ref):
    columns = mask_ref[...].reshape(CELLS, NZ).astype(F32).T
    return lambda r: jnp.broadcast_to(columns[:, r : r + 1], (NZ, R)).astype(BF)


def edges_kernel(
    state_hbm, cot_hbm, mask_ref, xlo_hbm, xhi_hbm, ylo_hbm, yhi_hbm, sxlo_hbm, sxhi_hbm,
    xlo, xhi, ylo, yhi, sxlo, sxhi, sem, out_sem,
):
    ends = ((0, NX - 1), (0, NY - 1))
    x_in = [
        pltpu.make_async_copy(cot_hbm.at[ends[0][i]], (xlo, xhi)[i], sem.at[i]) for i in range(2)
    ]
    y_in, s_in = [], []
    for i, face in enumerate((ylo, yhi)):
        y = ends[1][i]
        y_in.append(pltpu.make_async_copy(cot_hbm.at[:, y], face.at[1], sem.at[2 + 2 * i]))
        y_in.append(pltpu.make_async_copy(state_hbm.at[:, y], face.at[0], sem.at[3 + 2 * i]))
    for i, face in enumerate((sxlo, sxhi)):
        s_in.append(pltpu.make_async_copy(state_hbm.at[ends[0][i]], face, sem.at[6 + i]))
    pairs = ((xlo, xlo_hbm), (xhi, xhi_hbm), (ylo, ylo_hbm), (yhi, yhi_hbm), (sxlo, sxlo_hbm), (sxhi, sxhi_hbm))
    outs = [pltpu.make_async_copy(a, b, out_sem.at[i]) for i, (a, b) in enumerate(pairs)]
    for copy in x_in + y_in + s_in:
        copy.start()
    gate = mask_gate(mask_ref)
    for i, face in enumerate((xlo, xhi)):
        x_in[i].wait()
        for y in range(NY):
            face[y] = face[y] * gate(ends[0][i] * NY + y)
        outs[i].start()
    for i, face in enumerate((ylo, yhi)):
        y_in[2 * i].wait()
        y_in[2 * i + 1].wait()
        for x in range(NX):
            face[1, x] = face[1, x] * gate(x * NY + ends[1][i])
        outs[2 + i].start()
    for i in range(2):
        s_in[i].wait()
        outs[4 + i].start()
    for copy in outs:
        copy.wait()


x_face = jax.ShapeDtypeStruct((NY, NZ, R), BF)
y_face = jax.ShapeDtypeStruct((NX, NZ, R), BF)
two_y_faces = jax.ShapeDtypeStruct((2, NX, NZ, R), BF)


def edges(state, cotangent, mask):
    x, y = pltpu.VMEM((NY, NZ, R), BF), pltpu.VMEM((2, NX, NZ, R), BF)
    return pl.pallas_call(
        edges_kernel,
        out_shape=(x_face, x_face, two_y_faces, two_y_faces, x_face, x_face),
        in_specs=[hbm, hbm, whole],
        out_specs=(hbm,) * 6,
        scratch_shapes=[
            x, x, y, y, x, x, pltpu.SemaphoreType.DMA((8,)), pltpu.SemaphoreType.DMA((6,)),
        ],
        compiler_params=params(56),
        cost_estimate=cost(1 << 20, 6 << 20),
        name="edges",
    )(state, cotangent, mask)


PADDED = (NX + 2, NY + 2, NZ, R)
difference_arrays = [
    pltpu.VMEM((NX + 1, ROWS, R), BF),
    pltpu.VMEM((NX, ROWS + NZ, R), BF),
    pltpu.VMEM((NX, ROWS, R), BF),
    pltpu.VMEM((NX, ROWS, R), BF),
]
load_sems = pltpu.SemaphoreType.DMA((NX + 4,))
field_scratch = [pltpu.VMEM(PADDED, BF)] + difference_arrays + [load_sems]


def start_loads(padded, sem, centre, xlo, xhi, ylo, yhi):
    inside = pl.ds(1, NY)
    planes = pl.ds(1, NX)
    pairs = [
        (xlo, padded.at[0, inside]),
        (ylo, padded.at[planes, 0]),
        (yhi, padded.at[planes, NY + 1]),
    ]
    pairs += [(centre.at[p], padded.at[p + 1, inside]) for p in range(NX)]
    pairs.append((xhi, padded.at[NX + 1, inside]))
    copies = [pltpu.make_async_copy(a, b, sem.at[i]) for i, (a, b) in enumerate(pairs)]
    for copy in copies:
        copy.start()
    return copies


def wait_all(copies):
    for copy in copies:
        copy.wait()


GROUP = 4


def at_row(y):
    return pl.ds(pl.multiple_of(y * NZ, NZ), NZ)


def build(copies, padded, dx, dy, dzp, dzm, gates=None):
    place = lax.broadcasted_iota(jnp.int32, (NZ, R), 0)
    wait_all(copies[:3])
    for p in range(NX):
        copies[3 + p].wait()

        def some_rows(n, carry, p=p):
            y0 = n * GROUP
            below = padded[p + 1, y0]
            for j in range(GROUP):
                y = y0 + j
                centre = padded[p + 1, y + 1]
                if gates is not None:
                    centre = centre * gate_of(gates, p * NY + y).astype(BF)
                    padded[p + 1, y + 1] = centre
                dx[p, at_row(y), :] = centre - padded[p, y + 1]
                dy[p, at_row(y), :] = centre - below
                below = centre
                wide = centre.astype(F32)
                minus = wide - jnp.where(place > 0, pltpu.roll(wide, 1, 0), 0.0)
                plus = jnp.where(place < NZ - 1, pltpu.roll(minus, NZ - 1, 0), -wide)
                dzm[p, at_row(y), :] = minus.astype(BF)
                dzp[p, at_row(y), :] = plus.astype(BF)
            return carry

        lax.fori_loop(0, NY // GROUP, some_rows, 0)
        dy[p, ROWS : ROWS + NZ, :] = padded[p + 1, NY + 1] - padded[p + 1, NY]
    copies[NX + 3].wait()

    def last_plane(y, carry):
        dx[NX, at_row(y), :] = padded[NX + 1, y + 1] - padded[NX, y + 1]
        return carry

    lax.fori_loop(0, NY, last_plane, 0, unroll=4)


def pieces(p, dx, dy, dzp, dzm):
    return [
        dx[p + 1], dx[p], dy[p, NZ : NZ + ROWS, :], dy[p, 0:ROWS, :], dzp[p], dzm[p],
    ]


def times(p, differences, mats_ref):
    return jnp.dot(
        jnp.concatenate(pieces(p, *differences), axis=1), mats_ref[...],
        preferred_element_type=F32,
    )


def add_products(total, left, p, differences):
    turned = left.T
    for k, piece in enumerate(pieces(p, *differences)):
        total[:, k * 256 : k * 256 + 256] += jnp.dot(turned, piece, preferred_element_type=F32)


def fill_gates(gates, mask_ref):
    columns = mask_ref[...].reshape(CELLS, NZ).astype(F32).T
    for r in range(CELLS):
        gates[r] = jnp.broadcast_to(columns[:, r : r + 1], (NZ, 128))


def gate_of(gates, r):
    gate = gates[r]
    return jnp.concatenate([gate, gate], axis=1)


def inner_kernel(
    packed_ref, mask_ref, cot_ref, xlo_hbm, xhi_hbm, ylo_hbm, yhi_hbm,
    hi_ref, base_ref, hxlo_hbm, hxhi_hbm, hylo_hbm, hyhi_hbm, back_ref, flow_ref,
    dx, dy, dzp, dzm, padded, sem, gates, out_sem,
):
    copies = start_loads(padded, sem, cot_ref, xlo_hbm, xhi_hbm, ylo_hbm.at[1], yhi_hbm.at[1])
    fill_gates(gates, mask_ref)
    for k in range(6):
        a, b, c, e = load_packed(packed_ref, k)
        sign = 1.0 if k % 2 == 0 else -1.0
        other = k + 1 - 2 * (k % 2)
        for ref, at, s in ((back_ref, k * 256, sign), (flow_ref, other * 256, -sign)):
            ref[at : at + 128, :128] = (s * a).astype(BF)
            ref[at : at + 128, 128:] = (s * b).astype(BF)
            ref[at + 128 : at + 256, :128] = (s * c).astype(BF)
            ref[at + 128 : at + 256, 128:] = (s * e).astype(BF)
    differences = (dx, dy, dzp, dzm)
    build(copies, padded, *differences, gates=gates)

    def outs(p):
        return [
            pltpu.make_async_copy(hi_ref.at[p, 0], hylo_hbm.at[p], out_sem.at[0, p]),
            pltpu.make_async_copy(hi_ref.at[p, NY - 1], hyhi_hbm.at[p], out_sem.at[1, p]),
        ]

    first = pltpu.make_async_copy(hi_ref.at[0], hxlo_hbm, out_sem.at[2, 0])
    last = pltpu.make_async_copy(hi_ref.at[NX - 1], hxhi_hbm, out_sem.at[2, 1])

    def one_plane(p, carry):
        back = times(p, differences, back_ref)
        for y in range(NY):
            half = 0.5 * cot_ref[p, y].astype(F32)
            inner = half + (0.5 * courant) * back[y * NZ : (y + 1) * NZ, :]
            hi_ref[p, y] = (gate_of(gates, p * NY + y) * inner).astype(BF)
            base_ref[p, y] = half + inner
        for copy in outs(p):
            copy.start()

        @pl.when(p == 0)
        def _():
            first.start()

        return carry

    lax.fori_loop(0, NX, one_plane, 0)
    last.start()
    for p in range(NX):
        wait_all(outs(p))
    wait_all([first, last])


def inner_step(packed, cotangent, mask, xlo, xhi, ylo, yhi):
    return pl.pallas_call(
        inner_kernel,
        out_shape=(
            pltpu.VMEM(GRID, BF), pltpu.VMEM(GRID, F32),
            x_face, x_face, y_face, y_face, pltpu.VMEM((1536, 256), BF), pltpu.VMEM((1536, 256), BF),
        ) + tuple(difference_arrays),
        in_specs=[whole, whole, whole] + [raw] * 4,
        out_specs=(whole, whole) + (hbm,) * 4 + (whole,) * 6,
        scratch_shapes=[
            pltpu.VMEM(PADDED, BF),
            load_sems,
            pltpu.VMEM((CELLS, NZ, 128), F32),
            pltpu.SemaphoreType.DMA((3, NX)),
        ],
        compiler_params=params(20),
        cost_estimate=cost(2 * 4096 * 256 * 1536, 14 << 20),
        name="inner",
    )(packed, mask, cotangent, xlo, xhi, ylo, yhi)


def middle_kernel(
    flow_ref, mask_ref, state_ref, sxlo, sxhi, ylo, yhi, hdx, hdy, hdzp, hdzm,
    grads_ref, state_pad, sdx, sdy, sdzp, sdzm, sem_s, gates,
):
    state_copies = start_loads(state_pad, sem_s, state_ref, sxlo, sxhi, ylo.at[0], yhi.at[0])
    fill_gates(gates, mask_ref)
    grads_ref[...] = jnp.zeros_like(grads_ref)
    states, helds = (sdx, sdy, sdzp, sdzm), (hdx, hdy, hdzp, hdzm)
    build(state_copies, state_pad, *states)

    def one_plane(p, carry):
        flow = times(p, states, flow_ref)
        rows = []
        for y in range(NY):
            own = state_pad[p + 1, y + 1].astype(F32)
            moved = courant * flow[y * NZ : (y + 1) * NZ, :]
            rows.append((own + gate_of(gates, p * NY + y) * moved).astype(BF))
        for y in range(NY):
            state_pad[p + 1, y + 1] = rows[y]
        return carry

    lax.fori_loop(0, NX, one_plane, 0)

    def products(p, carry):
        middle = state_pad[p + 1, 1 : NY + 1].reshape(ROWS, R)
        add_products(grads_ref, middle, p, helds)
        return carry

    lax.fori_loop(0, NX, products, 0)


def middle_step(flow_mats, mask, state, state_x, y_halos, held_differences):
    return pl.pallas_call(
        middle_kernel,
        out_shape=pltpu.VMEM((256, 1536), F32),
        in_specs=[whole] * 3 + [raw] * 4 + [whole] * 4,
        out_specs=whole,
        scratch_shapes=field_scratch + [pltpu.VMEM((CELLS, NZ, 128), F32)],
        compiler_params=params(22),
        cost_estimate=cost(4 * 4096 * 256 * 1536, 4 << 20),
        name="middle",
    )(flow_mats, mask, state, *state_x, *y_halos, *held_differences)


def last_kernel(
    held_grads_ref, state_ref, hi_ref, back_ref, base_ref, xlo_hbm, xhi_hbm, ylo_hbm, yhi_hbm,
    packed_ref, out_hbm, padded, dx, dy, dzp, dzm, sem, total, out, out_sem,
):
    copies = start_loads(padded, sem, hi_ref, xlo_hbm, xhi_hbm, ylo_hbm, yhi_hbm)
    total[...] = 0.5 * held_grads_ref[...]
    differences = (dx, dy, dzp, dzm)
    build(copies, padded, *differences)

    def out_copy(p):
        return pltpu.make_async_copy(out.at[p], out_hbm.at[p], out_sem.at[p])

    def one_plane(p, carry):
        back = times(p, differences, back_ref)
        for y in range(NY):
            out[p, y] = (base_ref[p, y] + courant * back[y * NZ : (y + 1) * NZ, :]).astype(BF)
        out_copy(p).start()
        return carry

    lax.fori_loop(0, NX, one_plane, 0)

    def products(p, carry):
        add_products(total, state_ref[p].reshape(ROWS, R), p, differences)
        return carry

    lax.fori_loop(0, NX, products, 0)
    diagonals = []
    for k in range(6):
        scale = courant if k % 2 == 0 else -courant
        g = total.at[:, pl.ds(k * 256, 256)]
        a, b, c, d = g[:128, :128], g[:128, 128:], g[128:, :128], g[128:, 128:]
        diagonals.append(
            store_packed(packed_ref, k, scale * (a + a.T), scale * (b + c.T), scale * (d + d.T))
        )
    store_diagonals(packed_ref, diagonals)
    for p in range(NX):
        out_copy(p).wait()


def last_step(held_grads, state, hi, back_mats, base, xlo, xhi, ylo, yhi):
    return pl.pallas_call(
        last_kernel,
        out_shape=(jax.ShapeDtypeStruct((2048, 128), BF), jax.ShapeDtypeStruct(GRID, BF)),
        in_specs=[whole] * 5 + [raw] * 4,
        out_specs=(whole, hbm),
        scratch_shapes=field_scratch
        + [
            pltpu.VMEM((256, 1536), F32),
            pltpu.VMEM(GRID, BF),
            pltpu.SemaphoreType.DMA((NX,)),
        ],
        compiler_params=params(24),
        cost_estimate=cost(4 * 4096 * 256 * 1536, 5 << 20),
        name="last",
    )(held_grads, state, hi, back_mats, base, xlo, xhi, ylo, yhi)


CHUNK = 512


def weighted_kernel(factors_ref, speeds_ref, signs_ref, out_ref):
    rows = rate_rows(speeds_ref, signs_ref)
    columns = jnp.concatenate(rows + rows[:2], axis=0).T
    values = factors_ref[...].astype(F32)
    for k in range(6):
        rate = jnp.broadcast_to(columns[:, k : k + 1], (CHUNK, R))
        out_ref[:, k * 256 : k * 256 + 256] = (rate * values).astype(BF)


def weigh(factors, speeds, signs):
    rows = factors.shape[0]
    return pl.pallas_call(
        weighted_kernel,
        grid=(rows // CHUNK,),
        out_shape=jax.ShapeDtypeStruct((rows, 1536), BF),
        in_specs=[
            pl.BlockSpec((CHUNK, R), lambda i: (i, 0)),
            pl.BlockSpec((3, CHUNK), lambda i: (0, i)),
            pl.BlockSpec((3, CHUNK), lambda i: (0, i)),
        ],
        out_specs=pl.BlockSpec((CHUNK, 1536), lambda i: (i, 0)),
        compiler_params=params(56),
        cost_estimate=cost(2048 * 1536, 8 << 20),
        name="weigh",
    )(factors, speeds, signs)


def final_kernel(packed_ref, weighted_ref, out_ref, mats):
    @pl.when(pl.program_id(0) == 0)
    def _():
        for k in range(6):
            a, b, c, d = load_packed(packed_ref, k)
            at = k * 256
            mats[at : at + 128, :128] = a.astype(BF)
            mats[at : at + 128, 128:] = b.astype(BF)
            mats[at + 128 : at + 256, :128] = c.astype(BF)
            mats[at + 128 : at + 256, 128:] = d.astype(BF)

    out_ref[...] = jnp.dot(weighted_ref[...], mats[...], preferred_element_type=F32)


def constant(shape):
    return pl.BlockSpec(shape, lambda i: (0,) * len(shape), pipeline_mode=pl.Buffered(1))


def final_step(packed, weighted):
    rows = weighted.shape[0]
    return pl.pallas_call(
        final_kernel,
        grid=(rows // CHUNK,),
        out_shape=jax.ShapeDtypeStruct((rows, R), F32),
        in_specs=[constant((2048, 128)), pl.BlockSpec((CHUNK, 1536), lambda i: (i, 0))],
        out_specs=pl.BlockSpec((CHUNK, R), lambda i: (i, 0)),
        scratch_shapes=[pltpu.VMEM((1536, 256), BF)],
        compiler_params=params(58),
        cost_estimate=cost(2 * 2048 * 256 * 1536, 8 << 20),
        name="final",
    )(packed, weighted)


def shift(axis, lo, hi):
    count = lax.axis_size(axis)
    forward = [(i, i + 1) for i in range(count - 1)]
    backward = [(i + 1, i) for i in range(count - 1)]
    from_below = lax.ppermute(hi, axis, forward)
    from_above = lax.ppermute(lo, axis, backward)
    return from_below, from_above


Y_AXES = ("gy", "gz")


def near(x):
    return pltpu.with_memory_space_constraint(x, pltpu.VMEM)


def on_device(state, cotangent, factors, speeds, signs, mask):
    hxlo, hxhi, ylo, yhi, sxlo, sxhi = edges(state, cotangent, mask)
    speeds, hxlo, hxhi = lax.optimization_barrier((speeds, hxlo, hxhi))
    held_x = shift("gx", hxlo, hxhi)
    copies = scatter_sum(gram(factors, speeds, signs))
    y_halos = shift(Y_AXES, ylo, yhi)
    copies, sxlo, sxhi = lax.optimization_barrier((copies, sxlo, sxhi))
    state_x = shift("gx", sxlo, sxhi)
    packed = gather(copies)
    hi, base, hxlo, hxhi, hylo, hyhi, back_mats, flow_mats, *held_differences = inner_step(
        near(packed), near(cotangent), mask, *held_x, *y_halos
    )
    hi_halos = shift("gx", hxlo, hxhi) + shift(Y_AXES, hylo, hyhi)
    held_grads = middle_step(
        near(flow_mats), mask, near(state), state_x, y_halos, [near(d) for d in held_differences]
    )
    partial, grad_state = last_step(
        near(held_grads), near(state), near(hi), near(back_mats), near(base), *hi_halos
    )
    sums = scatter_sum(partial)
    weighted = weigh(factors, speeds, signs)
    symmetric = gather(sums)
    grad_factors = final_step(near(symmetric), weighted)
    return (grad_state, grad_factors)


def solution(mesh):
    placed = (
        P("gx", ("gy", "gz"), None, None),
        P("gx", ("gy", "gz"), None, None),
        P(ALL, None),
        P(None, ALL),
        P(None, ALL),
        P("gx", ("gy", "gz"), None),
    )

    return jax.shard_map(
        on_device,
        mesh=mesh,
        in_specs=placed,
        out_specs=(P("gx", ("gy", "gz"), None, None), P(ALL, None)),
        check_vma=False,
    )
```

```python
import jax
import jax.numpy as jnp
from jax import lax
from jax.experimental import pallas as pl
from jax.experimental.pallas import tpu as pltpu
from jax.sharding import PartitionSpec as P

courant = 0.2
ALL = ("gx", "gy", "gz")
BF = jnp.bfloat16
F32 = jnp.float32
NX, NY, NZ, R = 4, 8, 128, 256
ROWS = NY * NZ
whole = pl.BlockSpec(memory_space=pltpu.VMEM)
raw = pl.BlockSpec(memory_space=pl.ANY)
hbm = pl.BlockSpec(memory_space=pltpu.HBM)


def params(mib, **kw):
    return pltpu.CompilerParams(vmem_limit_bytes=mib * 1024 * 1024, **kw)


def cost(flops, bytes_accessed):
    return pl.CostEstimate(flops=flops, bytes_accessed=bytes_accessed, transcendentals=0)


def tri_masks():
    row = lax.broadcasted_iota(jnp.int32, (128, 128), 0)
    col = lax.broadcasted_iota(jnp.int32, (128, 128), 1)
    return row, col


def store_packed(out_ref, k, a, b, d):
    row, col = tri_masks()
    out_ref[k * 256 : k * 256 + 128, :] = jnp.where(row <= col, a, d).astype(BF)
    out_ref[k * 256 + 128 : k * 256 + 256, :] = b.astype(BF)
    return jnp.sum(jnp.where(row == col, d, 0.0), axis=0, keepdims=True)


def store_diagonals(out_ref, diagonals):
    zeros = jnp.zeros((10, 128), F32)
    out_ref[1536:1552, :] = jnp.concatenate(diagonals + [zeros], axis=0).astype(BF)
    out_ref[1552:2048, :] = jnp.zeros((496, 128), BF)


def load_packed(packed_ref, k):
    row, col = tri_masks()
    t = packed_ref[k * 256 : k * 256 + 128, :].astype(F32)
    b = packed_ref[k * 256 + 128 : k * 256 + 256, :].astype(F32)
    diag = packed_ref[1536:1552, :].astype(F32)[k : k + 1, :]
    tt = t.T
    a = jnp.where(row <= col, t, tt)
    d = jnp.where(row > col, t, jnp.where(row < col, tt, jnp.broadcast_to(diag, (128, 128))))
    return a, b, b.T, d


def rate_rows(speeds_ref, signs_ref):
    rows = []
    for d in range(3):
        chosen = signs_ref[d : d + 1, :].astype(F32)
        speed = speeds_ref[d : d + 1, :]
        rows.append(speed * chosen)
        rows.append(speed * (1.0 - chosen))
    return rows


def gram_kernel(factors_ref, speeds_ref, signs_ref, out_ref, turned_ref, acc_ref):
    rows = rate_rows(speeds_ref, signs_ref)
    turned = factors_ref[...].astype(F32).T
    for k in range(6):
        turned_ref[k * 256 : k * 256 + 256, :] = (turned * rows[k]).astype(BF)
    acc_ref[...] = jnp.dot(turned_ref[...], factors_ref[...], preferred_element_type=F32)
    diagonals = []
    for k in range(6):
        g = acc_ref.at[pl.ds(k * 256, 256), :]
        diagonals.append(
            store_packed(out_ref, k, g[:128, :128], g[:128, 128:], g[128:, 128:])
        )
    store_diagonals(out_ref, diagonals)


def gram(factors, speeds, signs):
    return pl.pallas_call(
        gram_kernel,
        out_shape=jax.ShapeDtypeStruct((2048, 128), BF),
        in_specs=[whole] * 3,
        out_specs=whole,
        scratch_shapes=[pltpu.VMEM((1536, 2048), BF), pltpu.VMEM((1536, 256), F32)],
        compiler_params=params(20),
        cost_estimate=cost(2 * 2048 * 256 * 1536, 2 << 20),
        name="gram",
    )(factors, speeds, signs)


def total_kernel(parts_ref, out_ref):
    total = jnp.sum(parts_ref[...].astype(F32), axis=0).astype(BF)
    out_ref[...] = jnp.broadcast_to(total[None], (128, 16, 128))


def scatter_sum(packed):
    pieces = packed.reshape(128, 16, 128)
    mine = lax.all_to_all(pieces, ALL, split_axis=0, concat_axis=0, tiled=True)
    return pl.pallas_call(
        total_kernel,
        out_shape=jax.ShapeDtypeStruct((128, 16, 128), BF),
        in_specs=[whole],
        out_specs=whole,
        compiler_params=params(4),
        cost_estimate=cost(1 << 18, 1 << 20),
        name="total",
    )(mine)


def gather(copies):
    everything = lax.all_to_all(copies, ALL, split_axis=0, concat_axis=0, tiled=True)
    return everything.reshape(2048, 128)


GRID = (NX, NY, NZ, R)
CELLS = NX * NY


def mask_gate(mask_ref):
    columns = mask_ref[...].reshape(CELLS, NZ).astype(F32).T
    return lambda r: jnp.broadcast_to(columns[:, r : r + 1], (NZ, R)).astype(BF)


def edges_kernel(
    state_hbm, cot_hbm, mask_ref, xlo_hbm, xhi_hbm, ylo_hbm, yhi_hbm, sxlo_hbm, sxhi_hbm,
    xlo, xhi, ylo, yhi, sxlo, sxhi, sem, out_sem,
):
    ends = ((0, NX - 1), (0, NY - 1))
    x_in = [
        pltpu.make_async_copy(cot_hbm.at[ends[0][i]], (xlo, xhi)[i], sem.at[i]) for i in range(2)
    ]
    y_in, s_in = [], []
    for i, face in enumerate((ylo, yhi)):
        y = ends[1][i]
        y_in.append(pltpu.make_async_copy(cot_hbm.at[:, y], face.at[1], sem.at[2 + 2 * i]))
        y_in.append(pltpu.make_async_copy(state_hbm.at[:, y], face.at[0], sem.at[3 + 2 * i]))
    for i, face in enumerate((sxlo, sxhi)):
        s_in.append(pltpu.make_async_copy(state_hbm.at[ends[0][i]], face, sem.at[6 + i]))
    pairs = ((xlo, xlo_hbm), (xhi, xhi_hbm), (ylo, ylo_hbm), (yhi, yhi_hbm), (sxlo, sxlo_hbm), (sxhi, sxhi_hbm))
    outs = [pltpu.make_async_copy(a, b, out_sem.at[i]) for i, (a, b) in enumerate(pairs)]
    for copy in x_in + y_in + s_in:
        copy.start()
    gate = mask_gate(mask_ref)
    for i, face in enumerate((xlo, xhi)):
        x_in[i].wait()
        for y in range(NY):
            face[y] = face[y] * gate(ends[0][i] * NY + y)
        outs[i].start()
    for i, face in enumerate((ylo, yhi)):
        y_in[2 * i].wait()
        y_in[2 * i + 1].wait()
        for x in range(NX):
            face[1, x] = face[1, x] * gate(x * NY + ends[1][i])
        outs[2 + i].start()
    for i in range(2):
        s_in[i].wait()
        outs[4 + i].start()
    for copy in outs:
        copy.wait()


x_face = jax.ShapeDtypeStruct((NY, NZ, R), BF)
y_face = jax.ShapeDtypeStruct((NX, NZ, R), BF)
two_y_faces = jax.ShapeDtypeStruct((2, NX, NZ, R), BF)


def edges(state, cotangent, mask):
    x, y = pltpu.VMEM((NY, NZ, R), BF), pltpu.VMEM((2, NX, NZ, R), BF)
    return pl.pallas_call(
        edges_kernel,
        out_shape=(x_face, x_face, two_y_faces, two_y_faces, x_face, x_face),
        in_specs=[hbm, hbm, whole],
        out_specs=(hbm,) * 6,
        scratch_shapes=[
            x, x, y, y, x, x, pltpu.SemaphoreType.DMA((8,)), pltpu.SemaphoreType.DMA((6,)),
        ],
        compiler_params=params(56),
        cost_estimate=cost(1 << 20, 6 << 20),
        name="edges",
    )(state, cotangent, mask)


PADDED = (NX + 2, NY + 2, NZ, R)
difference_arrays = [
    pltpu.VMEM((NX + 1, ROWS, R), BF),
    pltpu.VMEM((NX, ROWS + NZ, R), BF),
    pltpu.VMEM((NX, ROWS, R), BF),
    pltpu.VMEM((NX, ROWS, R), BF),
]
gate_array = pltpu.VMEM((CELLS, NZ, 128), F32)
load_sems = pltpu.SemaphoreType.DMA((NX + 4,))
field_scratch = [pltpu.VMEM(PADDED, BF)] + difference_arrays + [load_sems]


def start_loads(padded, sem, centre, xlo, xhi, ylo, yhi):
    inside = pl.ds(1, NY)
    planes = pl.ds(1, NX)
    pairs = [
        (xlo, padded.at[0, inside]),
        (ylo, padded.at[planes, 0]),
        (yhi, padded.at[planes, NY + 1]),
    ]
    pairs += [(centre.at[p], padded.at[p + 1, inside]) for p in range(NX)]
    pairs.append((xhi, padded.at[NX + 1, inside]))
    copies = [pltpu.make_async_copy(a, b, sem.at[i]) for i, (a, b) in enumerate(pairs)]
    for copy in copies:
        copy.start()
    return copies


def wait_all(copies):
    for copy in copies:
        copy.wait()


GROUP = 4


def at_row(y):
    return pl.ds(pl.multiple_of(y * NZ, NZ), NZ)


def build(copies, padded, dx, dy, dzp, dzm, gates=None):
    place = lax.broadcasted_iota(jnp.int32, (NZ, R), 0)
    wait_all(copies[:3])
    for p in range(NX):
        copies[3 + p].wait()

        def some_rows(n, carry, p=p):
            y0 = n * GROUP
            below = padded[p + 1, y0]
            for j in range(GROUP):
                y = y0 + j
                centre = padded[p + 1, y + 1]
                if gates is not None:
                    centre = centre * gate_of(gates, p * NY + y).astype(BF)
                    padded[p + 1, y + 1] = centre
                dx[p, at_row(y), :] = centre - padded[p, y + 1]
                dy[p, at_row(y), :] = centre - below
                below = centre
                wide = centre.astype(F32)
                minus = wide - jnp.where(place > 0, pltpu.roll(wide, 1, 0), 0.0)
                plus = jnp.where(place < NZ - 1, pltpu.roll(minus, NZ - 1, 0), -wide)
                dzm[p, at_row(y), :] = minus.astype(BF)
                dzp[p, at_row(y), :] = plus.astype(BF)
            return carry

        lax.fori_loop(0, NY // GROUP, some_rows, 0)
        dy[p, ROWS : ROWS + NZ, :] = padded[p + 1, NY + 1] - padded[p + 1, NY]
    copies[NX + 3].wait()

    def last_plane(y, carry):
        dx[NX, at_row(y), :] = padded[NX + 1, y + 1] - padded[NX, y + 1]
        return carry

    lax.fori_loop(0, NY, last_plane, 0, unroll=4)


def pieces(p, dx, dy, dzp, dzm):
    return [
        dx[p + 1], dx[p], dy[p, NZ : NZ + ROWS, :], dy[p, 0:ROWS, :], dzp[p], dzm[p],
    ]


def times(p, differences, mats_ref):
    return jnp.dot(
        jnp.concatenate(pieces(p, *differences), axis=1), mats_ref[...],
        preferred_element_type=F32,
    )


def add_products(total, left, p, differences):
    turned = left.T
    for k, piece in enumerate(pieces(p, *differences)):
        total[:, k * 256 : k * 256 + 256] += jnp.dot(turned, piece, preferred_element_type=F32)


def fill_gates(gates, mask_ref):
    columns = mask_ref[...].reshape(CELLS, NZ).astype(F32).T
    for r in range(CELLS):
        gates[r] = jnp.broadcast_to(columns[:, r : r + 1], (NZ, 128))


def gate_of(gates, r):
    gate = gates[r]
    return jnp.concatenate([gate, gate], axis=1)


def inner_kernel(
    packed_ref, mask_ref, cot_ref, xlo_hbm, xhi_hbm, ylo_hbm, yhi_hbm,
    hi_ref, base_ref, hxlo_hbm, hxhi_hbm, hylo_hbm, hyhi_hbm, back_ref, flow_ref,
    dx, dy, dzp, dzm, gates, padded, sem, out_sem,
):
    copies = start_loads(padded, sem, cot_ref, xlo_hbm, xhi_hbm, ylo_hbm.at[1], yhi_hbm.at[1])
    fill_gates(gates, mask_ref)
    for k in range(6):
        a, b, c, e = load_packed(packed_ref, k)
        sign = 1.0 if k % 2 == 0 else -1.0
        other = k + 1 - 2 * (k % 2)
        for ref, at, s in ((back_ref, k * 256, sign), (flow_ref, other * 256, -sign)):
            ref[at : at + 128, :128] = (s * a).astype(BF)
            ref[at : at + 128, 128:] = (s * b).astype(BF)
            ref[at + 128 : at + 256, :128] = (s * c).astype(BF)
            ref[at + 128 : at + 256, 128:] = (s * e).astype(BF)
    differences = (dx, dy, dzp, dzm)
    build(copies, padded, *differences, gates=gates)

    def outs(p):
        return [
            pltpu.make_async_copy(hi_ref.at[p, 0], hylo_hbm.at[p], out_sem.at[0, p]),
            pltpu.make_async_copy(hi_ref.at[p, NY - 1], hyhi_hbm.at[p], out_sem.at[1, p]),
        ]

    first = pltpu.make_async_copy(hi_ref.at[0], hxlo_hbm, out_sem.at[2, 0])
    last = pltpu.make_async_copy(hi_ref.at[NX - 1], hxhi_hbm, out_sem.at[2, 1])

    def one_plane(p, carry):
        back = times(p, differences, back_ref)
        for y in range(NY):
            half = 0.5 * cot_ref[p, y].astype(F32)
            inner = half + (0.5 * courant) * back[y * NZ : (y + 1) * NZ, :]
            hi_ref[p, y] = (gate_of(gates, p * NY + y) * inner).astype(BF)
            base_ref[p, y] = half + inner
        for copy in outs(p):
            copy.start()

        @pl.when(p == 0)
        def _():
            first.start()

        return carry

    lax.fori_loop(0, NX, one_plane, 0)
    last.start()
    for p in range(NX):
        wait_all(outs(p))
    wait_all([first, last])


def inner_step(packed, cotangent, mask, xlo, xhi, ylo, yhi):
    return pl.pallas_call(
        inner_kernel,
        out_shape=(
            pltpu.VMEM(GRID, BF), pltpu.VMEM(GRID, F32),
            x_face, x_face, y_face, y_face, pltpu.VMEM((1536, 256), BF), pltpu.VMEM((1536, 256), BF),
        ) + tuple(difference_arrays) + (gate_array,),
        in_specs=[whole, whole, whole] + [raw] * 4,
        out_specs=(whole, whole) + (hbm,) * 4 + (whole,) * 7,
        scratch_shapes=[pltpu.VMEM(PADDED, BF), load_sems, pltpu.SemaphoreType.DMA((3, NX))],
        compiler_params=params(20),
        cost_estimate=cost(2 * 4096 * 256 * 1536, 14 << 20),
        name="inner",
    )(packed, mask, cotangent, xlo, xhi, ylo, yhi)


def middle_kernel(
    flow_ref, state_ref, sxlo, sxhi, ylo, yhi, hdx, hdy, hdzp, hdzm, gates,
    grads_ref, state_pad, sdx, sdy, sdzp, sdzm, sem_s,
):
    state_copies = start_loads(state_pad, sem_s, state_ref, sxlo, sxhi, ylo.at[0], yhi.at[0])
    grads_ref[...] = jnp.zeros_like(grads_ref)
    states, helds = (sdx, sdy, sdzp, sdzm), (hdx, hdy, hdzp, hdzm)
    build(state_copies, state_pad, *states)

    def one_plane(p, carry):
        flow = times(p, states, flow_ref)
        rows = []
        for y in range(NY):
            own = state_pad[p + 1, y + 1].astype(F32)
            moved = courant * flow[y * NZ : (y + 1) * NZ, :]
            rows.append((own + gate_of(gates, p * NY + y) * moved).astype(BF))
        for y in range(NY):
            state_pad[p + 1, y + 1] = rows[y]
        return carry

    lax.fori_loop(0, NX, one_plane, 0)

    def products(p, carry):
        middle = state_pad[p + 1, 1 : NY + 1].reshape(ROWS, R)
        add_products(grads_ref, middle, p, helds)
        return carry

    lax.fori_loop(0, NX, products, 0)


def middle_step(flow_mats, state, state_x, y_halos, held_differences, gates):
    return pl.pallas_call(
        middle_kernel,
        out_shape=pltpu.VMEM((256, 1536), F32),
        in_specs=[whole] * 2 + [raw] * 4 + [whole] * 5,
        out_specs=whole,
        scratch_shapes=field_scratch,
        compiler_params=params(22),
        cost_estimate=cost(4 * 4096 * 256 * 1536, 4 << 20),
        name="middle",
    )(flow_mats, state, *state_x, *y_halos, *held_differences, gates)


def last_kernel(
    held_grads_ref, state_ref, hi_ref, back_ref, base_ref, xlo_hbm, xhi_hbm, ylo_hbm, yhi_hbm,
    packed_ref, out_hbm, padded, dx, dy, dzp, dzm, sem, total, out, out_sem,
):
    copies = start_loads(padded, sem, hi_ref, xlo_hbm, xhi_hbm, ylo_hbm, yhi_hbm)
    total[...] = 0.5 * held_grads_ref[...]
    differences = (dx, dy, dzp, dzm)
    build(copies, padded, *differences)

    def out_copy(p):
        return pltpu.make_async_copy(out.at[p], out_hbm.at[p], out_sem.at[p])

    def one_plane(p, carry):
        back = times(p, differences, back_ref)
        for y in range(NY):
            out[p, y] = (base_ref[p, y] + courant * back[y * NZ : (y + 1) * NZ, :]).astype(BF)
        out_copy(p).start()
        return carry

    lax.fori_loop(0, NX, one_plane, 0)

    def products(p, carry):
        add_products(total, state_ref[p].reshape(ROWS, R), p, differences)
        return carry

    lax.fori_loop(0, NX, products, 0)
    diagonals = []
    for k in range(6):
        scale = courant if k % 2 == 0 else -courant
        g = total.at[:, pl.ds(k * 256, 256)]
        a, b, c, d = g[:128, :128], g[:128, 128:], g[128:, :128], g[128:, 128:]
        diagonals.append(
            store_packed(packed_ref, k, scale * (a + a.T), scale * (b + c.T), scale * (d + d.T))
        )
    store_diagonals(packed_ref, diagonals)
    for p in range(NX):
        out_copy(p).wait()


def last_step(held_grads, state, hi, back_mats, base, xlo, xhi, ylo, yhi):
    return pl.pallas_call(
        last_kernel,
        out_shape=(jax.ShapeDtypeStruct((2048, 128), BF), jax.ShapeDtypeStruct(GRID, BF)),
        in_specs=[whole] * 5 + [raw] * 4,
        out_specs=(whole, hbm),
        scratch_shapes=field_scratch
        + [
            pltpu.VMEM((256, 1536), F32),
            pltpu.VMEM(GRID, BF),
            pltpu.SemaphoreType.DMA((NX,)),
        ],
        compiler_params=params(24),
        cost_estimate=cost(4 * 4096 * 256 * 1536, 5 << 20),
        name="last",
    )(held_grads, state, hi, back_mats, base, xlo, xhi, ylo, yhi)


CHUNK = 512


def weighted_kernel(factors_ref, speeds_ref, signs_ref, out_ref):
    rows = rate_rows(speeds_ref, signs_ref)
    columns = jnp.concatenate(rows + rows[:2], axis=0).T
    values = factors_ref[...].astype(F32)
    for k in range(6):
        rate = jnp.broadcast_to(columns[:, k : k + 1], (CHUNK, R))
        out_ref[:, k * 256 : k * 256 + 256] = (rate * values).astype(BF)


def weigh(factors, speeds, signs):
    rows = factors.shape[0]
    return pl.pallas_call(
        weighted_kernel,
        grid=(rows // CHUNK,),
        out_shape=jax.ShapeDtypeStruct((rows, 1536), BF),
        in_specs=[
            pl.BlockSpec((CHUNK, R), lambda i: (i, 0)),
            pl.BlockSpec((3, CHUNK), lambda i: (0, i)),
            pl.BlockSpec((3, CHUNK), lambda i: (0, i)),
        ],
        out_specs=pl.BlockSpec((CHUNK, 1536), lambda i: (i, 0)),
        compiler_params=params(56),
        cost_estimate=cost(2048 * 1536, 8 << 20),
        name="weigh",
    )(factors, speeds, signs)


def final_kernel(packed_ref, weighted_ref, out_ref, mats):
    @pl.when(pl.program_id(0) == 0)
    def _():
        for k in range(6):
            a, b, c, d = load_packed(packed_ref, k)
            at = k * 256
            mats[at : at + 128, :128] = a.astype(BF)
            mats[at : at + 128, 128:] = b.astype(BF)
            mats[at + 128 : at + 256, :128] = c.astype(BF)
            mats[at + 128 : at + 256, 128:] = d.astype(BF)

    out_ref[...] = jnp.dot(weighted_ref[...], mats[...], preferred_element_type=F32)


def constant(shape):
    return pl.BlockSpec(shape, lambda i: (0,) * len(shape), pipeline_mode=pl.Buffered(1))


def final_step(packed, weighted):
    rows = weighted.shape[0]
    return pl.pallas_call(
        final_kernel,
        grid=(rows // CHUNK,),
        out_shape=jax.ShapeDtypeStruct((rows, R), F32),
        in_specs=[constant((2048, 128)), pl.BlockSpec((CHUNK, 1536), lambda i: (i, 0))],
        out_specs=pl.BlockSpec((CHUNK, R), lambda i: (i, 0)),
        scratch_shapes=[pltpu.VMEM((1536, 256), BF)],
        compiler_params=params(58),
        cost_estimate=cost(2 * 2048 * 256 * 1536, 8 << 20),
        name="final",
    )(packed, weighted)


def shift(axis, lo, hi):
    count = lax.axis_size(axis)
    forward = [(i, i + 1) for i in range(count - 1)]
    backward = [(i + 1, i) for i in range(count - 1)]
    from_below = lax.ppermute(hi, axis, forward)
    from_above = lax.ppermute(lo, axis, backward)
    return from_below, from_above


Y_AXES = ("gy", "gz")


def near(x):
    return pltpu.with_memory_space_constraint(x, pltpu.VMEM)


def on_device(state, cotangent, factors, speeds, signs, mask):
    hxlo, hxhi, ylo, yhi, sxlo, sxhi = edges(state, cotangent, mask)
    speeds, hxlo, hxhi = lax.optimization_barrier((speeds, hxlo, hxhi))
    held_x = shift("gx", hxlo, hxhi)
    copies = scatter_sum(gram(factors, speeds, signs))
    y_halos = shift(Y_AXES, ylo, yhi)
    copies, sxlo, sxhi = lax.optimization_barrier((copies, sxlo, sxhi))
    state_x = shift("gx", sxlo, sxhi)
    packed = gather(copies)
    hi, base, hxlo, hxhi, hylo, hyhi, back_mats, flow_mats, *left = inner_step(
        near(packed), near(cotangent), mask, *held_x, *y_halos
    )
    hi_halos = shift("gx", hxlo, hxhi) + shift(Y_AXES, hylo, hyhi)
    *held_differences, gates = [near(array) for array in left]
    held_grads = middle_step(
        near(flow_mats), near(state), state_x, y_halos, held_differences, gates
    )
    partial, grad_state = last_step(
        near(held_grads), near(state), near(hi), near(back_mats), near(base), *hi_halos
    )
    sums = scatter_sum(partial)
    weighted = weigh(factors, speeds, signs)
    symmetric = gather(sums)
    grad_factors = final_step(near(symmetric), weighted)
    return (grad_state, grad_factors)


def solution(mesh):
    placed = (
        P("gx", ("gy", "gz"), None, None),
        P("gx", ("gy", "gz"), None, None),
        P(ALL, None),
        P(None, ALL),
        P(None, ALL),
        P("gx", ("gy", "gz"), None),
    )

    return jax.shard_map(
        on_device,
        mesh=mesh,
        in_specs=placed,
        out_specs=(P("gx", ("gy", "gz"), None, None), P(ALL, None)),
        check_vma=False,
    )
```
